256 devices in a mesh: seq: 64 (over y, z, core), tensor: 4 (over x).
Axes of the slice: x: 4, y: 4, z: 8, core: 2. Of those that a mesh axis runs over, the one named last changes fastest.
Arguments:
- tokens: bfloat16 [32768, 3840], P('seq', 'tensor'), may hold values from -6 to 6
- w_query: bfloat16 [3840, 2048], P(None, 'tensor'), may hold values from -0.09375 to 0.09375
- w_key: bfloat16 [3840, 1024], P(None, 'tensor'), may hold values from -0.09375 to 0.09375
- w_value: bfloat16 [3840, 1024], P(None, 'tensor'), may hold values from -0.09375 to 0.09375
- query_gain: float32 [256], replicated, may hold values from 0.1 to 1.9
- key_gain: float32 [256], replicated, may hold values from 0.1 to 1.9
- adapter_down: bfloat16 [64, 64, 3840], P('seq', None, 'tensor'), may hold values from -0.09375 to 0.09375
- adapter_up: bfloat16 [64, 64, 2048], P('seq', None, 'tensor'), may hold values from -0.75 to 0.75
- adapter_ids: int32 [32768, 1], P('seq'), may hold values from 0 to 63; in each aligned block of 512 rows (0 to 511, 512 to 1023, ...) at most 16 rows name the same one
- doc_ids: int32 [32768], P('seq'), may hold values from 0 to 63, never falling along the last dimension, each value on 1 to 4096 neighbouring positions
- cotangent: bfloat16 [32768, 2048], P('seq', 'tensor'), may hold values from -6 to 6
Outputs:
- attended: bfloat16 [32768, 2048], P('seq', 'tensor')
- grad_up: float32 [64, 64, 2048], P('seq', None, 'tensor')
The draws below stay inside these ranges and needn't reach their ends.
Inputs may be any that keep to these rules, and one draw needn't show every extreme that they name: `adapter_ids`: within the 512 tokens of one device no adapter is named by more than 16 tokens; in every draw some adapter is named by exactly 16 tokens of some device. `doc_ids`: document numbers never fall along the slab; each document has 1 to 4096 tokens and one has exactly 4096.
All inputs are finite; a program needn't handle non-finite values.
Results may differ from the reference program's by a relative error of at most 0.0088.
Values may be sent and summed in bfloat16 or wider, within the bound.
A program may use at most 128 MiB of HBM per device.

```python
import math
import jax
import jax.numpy as jnp
import numpy as np
from jax import lax

D = 3840
HQ = 8
HK = 4
HD = 256
R = 64
WINDOW = 1024
ADAPTERS = 64
TOK_DEV = 512
TOKENS = 32768
DOCS = 64
MOST_DOC = 4096
CAP = 16
REACH = 2
N_SEQ = 64


def block_levels(stream_key, shape, pieces, smallest, high):
    level = 1.0
    for axis_at, shards_of in pieces:
        heights = jax.random.uniform(jax.random.fold_in(jax.random.fold_in(stream_key, 6), axis_at), (shards_of,), jnp.float32, smallest / len(pieces), high / len(pieces))
        level = level * jnp.repeat(jnp.exp(heights), shape[axis_at] // shards_of).reshape((-1,) + (1,) * (len(shape) - 1 - axis_at))
    return level


def length_profile(count, total, reach, skew):
    weights = [(1 << 20) // math.isqrt(standing ** skew) + 1 for standing in range(2, count + 1)]
    spare, given = total - reach - (count - 1), [1] * (count - 1)
    while spare > 0:
        candidates = [i for i in range(count - 1) if given[i] < reach]
        mass, budget = sum([weights[i] for i in candidates]), spare
        for i in candidates:
            extra = min(reach - given[i], max(1, budget * weights[i] // mass), spare)
            given[i] = given[i] + extra
            spare = spare - extra
    return np.array([reach] + given)


def ragged_sizes(stream_key, count, total, reach, skew):
    if count == 2:
        one = jax.random.randint(stream_key, (), max(1, total - reach), min(reach, total - 1) + 1)
        return jnp.stack([one, total - one])
    sizes = jnp.asarray(length_profile(count, total, reach, skew), jnp.int32)
    couples = (count - 1) // 2
    donor, receiver = sizes[1:1 + 2 * couples:2], sizes[2:2 + 2 * couples:2]
    slack = jnp.minimum(donor - 1, reach - receiver)
    passed = jax.random.randint(jax.random.fold_in(stream_key, 1), (couples,), 0, 1 << 20) % (slack + 1)
    sizes = sizes.at[1:1 + 2 * couples:2].set(donor - passed).at[2:2 + 2 * couples:2].set(receiver + passed)
    return sizes[jax.random.permutation(jax.random.fold_in(stream_key, 2), count)]


def deal_out(own_key, own, number, rows, number_of, top, bound, lean):
    ranking = jax.random.permutation(own_key, number_of)
    crowded, usual = shares(number_of, rows * top, bound, lean, True), shares(number_of, rows * top, bound, lean, False)
    places = jnp.arange(number_of)

    def named(lengths, rotation):
        used = int((lengths > 0).sum())
        fixed = max(1, used // 4)
        moved = fixed + (places - fixed + rotation * (used - fixed)) % max(1, number_of - fixed)
        return jnp.zeros((number_of,), jnp.int32).at[ranking[jnp.where(places < fixed, places, moved)]].set(jnp.asarray(lengths, jnp.int32))

    lengths = jnp.where(number % 4 == 0, named(crowded, number // 4), named(usual, number - number // 4 - 1))
    mixed = jax.random.permutation(jax.random.fold_in(own, 3), number_of)
    giver, sink = mixed[0:number_of // 2 * 2:2], mixed[1:number_of // 2 * 2:2]
    margin = jnp.minimum(lengths[giver] - 1, bound - lengths[sink]) // 2
    margin = jnp.where((giver == ranking[0]) | (sink == ranking[0]) | (lengths[sink] == 0), 0, jnp.maximum(margin, 0))
    moved = jax.random.randint(jax.random.fold_in(own, 4), (number_of // 2,), 0, 1 << 20) % (margin + 1)
    lengths = lengths.at[giver].add(-moved).at[sink].add(moved)
    members = jnp.searchsorted(jnp.cumsum(lengths), jnp.arange(rows * top), side="right").astype(jnp.int32)
    table = members.reshape(top, rows).T
    table = table[jax.random.permutation(jax.random.fold_in(own, 1), rows)]
    rotation = jax.random.randint(jax.random.fold_in(own, 2), (rows, 1), 0, top)
    return jnp.take_along_axis(table, (jnp.arange(top)[None, :] + rotation) % top, axis=1)


def shares(count, total, reach, skew, full):
    portions = [(1 << 20) // math.isqrt(grade ** skew) + 1 for grade in range(1, count + 1)]
    largest = reach if full else min(reach, max(-(-total // count), total * portions[0] // sum(portions)))
    least = 1 if total - largest >= count - 1 else 0
    counts, surplus = [largest] + [least] * (count - 1), total - largest - least * (count - 1)
    while surplus > 0:
        movable = [i for i in range(1, count) if counts[i] < largest] or [i for i in range(1, count) if counts[i] < reach]
        pool, budget = sum([portions[i] for i in movable]), surplus
        for i in movable:
            more = min(reach - counts[i], max(1, budget * portions[i] // pool), surplus)
            counts[i] = counts[i] + more
            surplus = surplus - more
    return np.array(counts)


def noise(key, shape, spread, bound, pieces=(), held_as=jnp.bfloat16):
    factor_of = block_levels(key, shape, pieces, -0.22, 0.18) if pieces else 1.0
    array = jax.random.normal(key, shape, jnp.float32) * spread * factor_of
    return jnp.minimum(jnp.maximum(array, -bound), bound).astype(held_as)


def setup_inputs(seed: int = 0) -> dict:
    seeds = jax.random.split(jax.random.key(seed), 12)
    tokens = noise(seeds[0], (TOKENS, D), 1.0, 6.0, ((0, 64), (1, 4)))
    w_query = noise(seeds[1], (D, HQ * HD), D ** -0.5, 0.09375, ((1, 4),))
    w_key = noise(seeds[2], (D, HK * HD), D ** -0.5, 0.09375, ((1, 4),))
    w_value = noise(seeds[3], (D, HK * HD), D ** -0.5, 0.09375, ((1, 4),))
    query_gain = jnp.clip(1.0 + 0.18 * jax.random.normal(seeds[4], (HD,), jnp.float32), 0.1, 1.9)
    key_gain = jnp.clip(1.0 + 0.18 * jax.random.normal(seeds[5], (HD,), jnp.float32), 0.1, 1.9)
    adapter_down = noise(seeds[6], (ADAPTERS, R, D), D ** -0.5, 0.09375, ((0, 64), (2, 4)))
    adapter_up = noise(seeds[7], (ADAPTERS, R, HQ * HD), R ** -0.5, 0.75, ((0, 64), (2, 4)))
    adapter_ids_keys = jax.random.split(jax.random.fold_in(seeds[8], 1), TOKENS // TOK_DEV)
    adapter_ids_turns = jax.random.permutation(jax.random.fold_in(seeds[8], 3), TOKENS // TOK_DEV)
    adapter_ids = jax.vmap(lambda own, number: deal_out(jax.random.fold_in(seeds[8], 2), own, number, TOK_DEV, ADAPTERS, 1, CAP, 2))(adapter_ids_keys, adapter_ids_turns).reshape((TOKENS, 1))
    doc_ids = jnp.searchsorted(jnp.cumsum(ragged_sizes(seeds[9], DOCS, TOKENS, MOST_DOC, 1)), jnp.arange(TOKENS), side="right").astype(jnp.int32)
    cotangent = noise(seeds[10], (TOKENS, HQ * HD), 1.0, 6.0, ((0, 64), (1, 4)))
    return dict(tokens=tokens, w_query=w_query, w_key=w_key, w_value=w_value, query_gain=query_gain, key_gain=key_gain, adapter_down=adapter_down, adapter_up=adapter_up, adapter_ids=adapter_ids, doc_ids=doc_ids, cotangent=cotangent)


def normalize(pre_field, gain_vec):
    mean_sq = lax.optimization_barrier(jnp.mean(pre_field * pre_field, axis=-1, keepdims=True))
    return pre_field * lax.rsqrt(mean_sq + 1e-06) * gain_vec

def rotate(pre_field, positions):
    half_dim = pre_field.shape[-1] // 2
    frequency = jnp.exp(jnp.arange(half_dim, dtype=jnp.float32) * (-2.0 * math.log(10000.0) / pre_field.shape[-1]))
    angles = positions.astype(jnp.float32)[:, None] * frequency[None, :]
    cosine = jnp.cos(angles)[:, None, :]
    sine_part = jnp.sin(angles)[:, None, :]
    lower_half = pre_field[..., :half_dim]
    second = pre_field[..., half_dim:]
    return jnp.concatenate([lower_half * cosine - second * sine_part, second * cosine + lower_half * sine_part], axis=-1)

def shape_query(pre_field, gain_vec, positions):
    return rotate(normalize(pre_field, gain_vec), positions)

def attend(queries, key_rows, values, upstream, allowed):
    score_scale = 1.0 / math.sqrt(queries.shape[-1])
    query_f = queries.astype(jnp.float32)
    key_f = key_rows.astype(jnp.float32)
    value_f = values.astype(jnp.float32)
    upstream_f = upstream.astype(jnp.float32)
    scores = jnp.einsum('tngd,knd->ngtk', query_f, key_f) * score_scale
    weights = jnp.where(allowed[None, None], jnp.exp(scores), 0.0)
    probs = weights / lax.optimization_barrier(jnp.sum(weights, axis=-1, keepdims=True))
    probs_low = lax.optimization_barrier(probs.astype(jnp.bfloat16))
    attended = jnp.einsum('ngtk,knd->tngd', probs_low.astype(jnp.float32), value_f)
    dprobs = jnp.einsum('tngd,knd->ngtk', upstream_f, value_f)
    delta = lax.optimization_barrier(jnp.sum(probs * dprobs, axis=-1, keepdims=True))
    dscores = lax.optimization_barrier((probs * (dprobs - delta) * score_scale).astype(jnp.bfloat16))
    dqueries = jnp.einsum('ngtk,knd->tngd', dscores.astype(jnp.float32), key_f)
    return (attended.astype(jnp.bfloat16), dqueries)

def reference(tokens, w_query, w_key, w_value, query_gain, key_gain, adapter_down, adapter_up, adapter_ids, doc_ids, cotangent):
    token_adapter = adapter_ids[:, 0]
    q_width = HQ * HD
    most_rows = N_SEQ * CAP
    padded = jnp.concatenate([tokens, jnp.zeros((1, D), tokens.dtype)], axis=0)

    def route_adapter(state_pair, adapter):
        lowrank, lifted = state_pair
        picked = jnp.nonzero(token_adapter == adapter, size=most_rows, fill_value=TOKENS)[0].astype(jnp.int32)
        slot_rows = padded[picked]
        down_rows = lax.dynamic_index_in_dim(adapter_down, adapter, 0, keepdims=False)
        up_matrix = lax.dynamic_index_in_dim(adapter_up, adapter, 0, keepdims=False)
        low_rows = jnp.dot(slot_rows, down_rows.T, preferred_element_type=jnp.float32).astype(jnp.bfloat16)
        lift_rows = jnp.dot(low_rows, up_matrix, preferred_element_type=jnp.float32).astype(jnp.bfloat16)
        lowrank = lowrank.at[picked].set(low_rows, mode='drop')
        lifted = lifted.at[picked].set(lift_rows, mode='drop')
        return ((lowrank, lifted), None)
    initial = (jnp.zeros((TOKENS, R), jnp.bfloat16), jnp.zeros((TOKENS, q_width), jnp.bfloat16))
    (lowrank, lifted), unused = lax.scan(route_adapter, initial, jnp.arange(ADAPTERS, dtype=jnp.int32))
    positions = jnp.arange(TOKENS, dtype=jnp.int32)
    query_pre = jnp.dot(tokens, w_query, preferred_element_type=jnp.float32) + lifted.astype(jnp.float32)
    query_pre = query_pre.reshape(TOKENS, HQ, HD)
    queries, query_back = jax.vjp(lambda pre_query: shape_query(pre_query, query_gain, positions), query_pre)
    queries = queries.astype(jnp.bfloat16)
    key_lin = jnp.dot(tokens, w_key, preferred_element_type=jnp.float32).reshape(TOKENS, HK, HD)
    key_rows = shape_query(key_lin, key_gain, positions).astype(jnp.bfloat16)
    values = jnp.dot(tokens, w_value, preferred_element_type=jnp.float32).astype(jnp.bfloat16).reshape(TOKENS, HK, HD)
    head_group = HQ // HK
    lead_len = REACH * TOK_DEV
    key_span = (REACH + 1) * TOK_DEV
    keys_pad = jnp.concatenate([jnp.zeros((lead_len, HK, HD), jnp.bfloat16), key_rows], axis=0)
    values_pad = jnp.concatenate([jnp.zeros((lead_len, HK, HD), jnp.bfloat16), values], axis=0)
    docs_pad = jnp.concatenate([jnp.zeros((lead_len,), jnp.int32), doc_ids.astype(jnp.int32)], axis=0)

    def query_block(block_index):
        first_row = block_index * TOK_DEV
        query_part = lax.dynamic_slice_in_dim(queries, first_row, TOK_DEV, 0).reshape(TOK_DEV, HK, head_group, HD)
        upstream = lax.dynamic_slice_in_dim(cotangent, first_row, TOK_DEV, 0).reshape(TOK_DEV, HK, head_group, HD)
        key_part = lax.dynamic_slice_in_dim(keys_pad, first_row, key_span, 0)
        value_part = lax.dynamic_slice_in_dim(values_pad, first_row, key_span, 0)
        key_docs = lax.dynamic_slice_in_dim(docs_pad, first_row, key_span, 0)
        query_docs = lax.dynamic_slice_in_dim(doc_ids.astype(jnp.int32), first_row, TOK_DEV, 0)
        query_pos = first_row + jnp.arange(TOK_DEV, dtype=jnp.int32)
        key_pos = first_row - lead_len + jnp.arange(key_span, dtype=jnp.int32)
        key_gap = query_pos[:, None] - key_pos[None, :]
        allowed = (query_docs[:, None] == key_docs[None, :]) & (key_gap >= 0) & (key_gap < WINDOW) & (key_pos[None, :] >= 0)
        block_out, block_grad = attend(query_part, key_part, value_part, upstream, allowed)
        return (block_out.reshape(TOK_DEV, q_width), block_grad.reshape(TOK_DEV, HQ, HD))
    outputs, dqueries = lax.map(query_block, jnp.arange(N_SEQ, dtype=jnp.int32))
    attended = outputs.reshape(TOKENS, q_width)
    dquery_pre, = query_back(dqueries.reshape(TOKENS, HQ, HD))
    dquery_pre = dquery_pre.reshape(TOKENS, q_width).astype(jnp.bfloat16)
    low_pad = jnp.concatenate([lowrank, jnp.zeros((1, R), jnp.bfloat16)], axis=0)
    grad_pad = jnp.concatenate([dquery_pre, jnp.zeros((1, q_width), jnp.bfloat16)], axis=0)

    def collect(adapter):
        picked = jnp.nonzero(token_adapter == adapter, size=most_rows, fill_value=TOKENS)[0].astype(jnp.int32)
        return jnp.dot(low_pad[picked].T, grad_pad[picked], preferred_element_type=jnp.float32)
    grad_up = lax.map(collect, jnp.arange(ADAPTERS, dtype=jnp.int32))
    return (attended, grad_up)
```

```python
import math

import jax
import jax.numpy as jnp
from jax import lax
from jax.sharding import PartitionSpec as P

HD = 256
R = 64
WINDOW = 1024
ADAPTERS = 64
CAP = 16


def passed_along(value, axis, steps):
    count = lax.axis_size(axis)
    first, last = (max(0, -steps), min(count, count - steps))
    return lax.ppermute(value, axis, [(source, source + steps) for source in range(first, last)])


def normalize(pre_field, gain_vec):
    mean_sq = jnp.mean(pre_field * pre_field, axis=-1, keepdims=True)
    return pre_field * lax.rsqrt(mean_sq + 1e-06) * gain_vec


def rotate(pre_field, positions):
    half_dim = pre_field.shape[-1] // 2
    frequency = jnp.exp(
        jnp.arange(half_dim, dtype=jnp.float32) * (-2.0 * math.log(10000.0) / pre_field.shape[-1])
    )
    angles = positions.astype(jnp.float32)[:, None] * frequency[None, :]
    cosine = jnp.cos(angles)[:, None, :]
    sine_part = jnp.sin(angles)[:, None, :]
    lower_half = pre_field[..., :half_dim]
    second = pre_field[..., half_dim:]
    return jnp.concatenate(
        [lower_half * cosine - second * sine_part, second * cosine + lower_half * sine_part],
        axis=-1,
    )


def shape_query(pre_field, gain_vec, positions):
    return rotate(normalize(pre_field, gain_vec), positions)


def attend(queries, key_rows, values, upstream, allowed):
    score_scale = 1.0 / math.sqrt(queries.shape[-1])
    scores = (
        jnp.einsum("tngd,knd->ngtk", queries, key_rows, preferred_element_type=jnp.float32)
        * score_scale
    )
    weights = jnp.where(allowed[None, None], jnp.exp(scores), 0.0)
    probs = weights / jnp.sum(weights, axis=-1, keepdims=True)
    probs_low = probs.astype(jnp.bfloat16)
    attended = jnp.einsum("ngtk,knd->tngd", probs_low, values, preferred_element_type=jnp.float32)
    dprobs = jnp.einsum("tngd,knd->ngtk", upstream, values, preferred_element_type=jnp.float32)
    delta = jnp.sum(probs * dprobs, axis=-1, keepdims=True)
    dscores = (probs * (dprobs - delta) * score_scale).astype(jnp.bfloat16)
    dqueries = jnp.einsum("ngtk,knd->tngd", dscores, key_rows, preferred_element_type=jnp.float32)
    return (attended.astype(jnp.bfloat16), dqueries)


def local(
    tokens,
    w_query,
    w_key,
    w_value,
    query_gain,
    key_gain,
    adapter_down,
    adapter_up,
    adapter_ids,
    doc_ids,
    cotangent,
):
    tok_count = tokens.shape[0]
    feat_width = tokens.shape[1]
    q_width = w_query.shape[1]
    kv_width = w_key.shape[1]
    local_heads = q_width // HD
    kv_heads = kv_width // HD
    head_group = local_heads // kv_heads
    positions = lax.axis_index("seq") * tok_count + jnp.arange(tok_count, dtype=jnp.int32)
    shard_cols = lax.all_gather(tokens, "tensor", axis=1, tiled=True)
    query_lin = jnp.dot(shard_cols, w_query, preferred_element_type=jnp.float32)
    key_lin = jnp.dot(shard_cols, w_key, preferred_element_type=jnp.float32)
    value_lin = jnp.dot(shard_cols, w_value, preferred_element_type=jnp.float32)
    token_adapter = adapter_ids[:, 0]
    chosen = token_adapter[:, None] == jnp.arange(ADAPTERS, dtype=jnp.int32)[None, :]
    before = jnp.cumsum(chosen.astype(jnp.int32), axis=0) - 1
    slot_rank = jnp.sum(jnp.where(chosen, before, 0), axis=1)
    slot_index = token_adapter * CAP + slot_rank
    dispatch = (slot_index[None, :] == jnp.arange(ADAPTERS * CAP, dtype=jnp.int32)[:, None]).astype(
        jnp.bfloat16
    )
    outgoing = jnp.dot(dispatch, tokens, preferred_element_type=jnp.float32).astype(jnp.bfloat16)
    seq_count = lax.axis_size("seq")
    own_adapters = adapter_down.shape[0]
    arrived = lax.all_to_all(outgoing, "seq", 0, 0, tiled=True).reshape(
        seq_count, own_adapters, CAP, feat_width
    )
    partial_low = jnp.einsum(
        "sacd,ard->sacr", arrived, adapter_down, preferred_element_type=jnp.float32
    )
    slot_low = lax.psum(partial_low, "tensor").astype(jnp.bfloat16)
    slot_lift = jnp.einsum(
        "sacr,are->sace", slot_low, adapter_up, preferred_element_type=jnp.float32
    ).astype(jnp.bfloat16)
    back_lift = lax.all_to_all(
        slot_lift.reshape(seq_count * own_adapters * CAP, q_width), "seq", 0, 0, tiled=True
    )
    lifted = jnp.einsum(
        "st,se->te",
        dispatch,
        back_lift,
        preferred_element_type=jnp.float32,
    ).astype(jnp.bfloat16)
    query_pre = (query_lin + lifted.astype(jnp.float32)).reshape(tok_count, local_heads, HD)
    queries, query_back = jax.vjp(
        lambda pre_query: shape_query(pre_query, query_gain, positions), query_pre
    )
    queries = queries.astype(jnp.bfloat16).reshape(tok_count, kv_heads, head_group, HD)
    key_rows = shape_query(key_lin.reshape(tok_count, kv_heads, HD), key_gain, positions).astype(
        jnp.bfloat16
    )
    values = value_lin.astype(jnp.bfloat16).reshape(tok_count, kv_heads, HD)
    rim_count = WINDOW // tok_count
    key_list = []
    value_list = []
    doc_list = []
    place_list = []
    for distance in range(rim_count, 0, -1):
        far_keys, far_values, far_docs = passed_along((key_rows, values, doc_ids), "seq", distance)
        key_list.append(far_keys)
        value_list.append(far_values)
        doc_list.append(far_docs)
        place_list.append(positions - distance * tok_count)
    key_list.append(key_rows)
    value_list.append(values)
    doc_list.append(doc_ids)
    place_list.append(positions)
    window_keys = jnp.concatenate(key_list, axis=0)
    window_values = jnp.concatenate(value_list, axis=0)
    key_docs = jnp.concatenate(doc_list, axis=0)
    key_pos = jnp.concatenate(place_list, axis=0)
    key_gap = positions[:, None] - key_pos[None, :]
    allowed = (
        (doc_ids[:, None] == key_docs[None, :])
        & (key_gap >= 0)
        & (key_gap < WINDOW)
        & (key_pos[None, :] >= 0)
    )
    upstream = cotangent.reshape(tok_count, kv_heads, head_group, HD)
    block_out, dqueries = attend(queries, window_keys, window_values, upstream, allowed)
    attended = block_out.reshape(tok_count, q_width)
    (dquery_pre,) = query_back(dqueries.reshape(tok_count, local_heads, HD))
    dquery_pre = dquery_pre.reshape(tok_count, q_width).astype(jnp.bfloat16)
    out_grad = jnp.dot(dispatch, dquery_pre, preferred_element_type=jnp.float32).astype(
        jnp.bfloat16
    )
    grad_rows = lax.all_to_all(out_grad, "seq", 0, 0, tiled=True).reshape(
        seq_count, own_adapters, CAP, q_width
    )
    grad_up = jnp.einsum(
        "sacr,sace->are", slot_low, grad_rows, preferred_element_type=jnp.float32
    )
    return (attended, grad_up)


def solution(mesh):
    in_specs = (
        P("seq", "tensor"),
        P(None, "tensor"),
        P(None, "tensor"),
        P(None, "tensor"),
        P(),
        P(),
        P("seq", None, "tensor"),
        P("seq", None, "tensor"),
        P("seq", None),
        P("seq"),
        P("seq", "tensor"),
    )
    out_specs = (P("seq", "tensor"), P("seq", None, "tensor"))
    return jax.shard_map(local, mesh=mesh, in_specs=in_specs, out_specs=out_specs, check_vma=False)
```

```python
import math

import jax
import jax.numpy as jnp
from jax import lax
from jax.sharding import PartitionSpec as P

HD = 256
R = 64
WINDOW = 1024
ADAPTERS = 64
CAP = 16


def passed_along(value, axis, steps):
    count = lax.axis_size(axis)
    first, last = (max(0, -steps), min(count, count - steps))
    return lax.ppermute(value, axis, [(source, source + steps) for source in range(first, last)])


def normalize(pre_field, gain_vec):
    mean_sq = jnp.mean(pre_field * pre_field, axis=-1, keepdims=True)
    return pre_field * lax.rsqrt(mean_sq + 1e-06) * gain_vec


def rotate(pre_field, positions):
    half_dim = pre_field.shape[-1] // 2
    frequency = jnp.exp(
        jnp.arange(half_dim, dtype=jnp.float32) * (-2.0 * math.log(10000.0) / pre_field.shape[-1])
    )
    angles = positions.astype(jnp.float32)[:, None] * frequency[None, :]
    cosine = jnp.cos(angles)[:, None, :]
    sine_part = jnp.sin(angles)[:, None, :]
    lower_half = pre_field[..., :half_dim]
    second = pre_field[..., half_dim:]
    return jnp.concatenate(
        [lower_half * cosine - second * sine_part, second * cosine + lower_half * sine_part],
        axis=-1,
    )


def shape_query(pre_field, gain_vec, positions):
    return rotate(normalize(pre_field, gain_vec), positions)


def attend(queries, key_rows, values, upstream, allowed):
    score_scale = 1.0 / math.sqrt(queries.shape[-1])
    scores = (
        jnp.einsum("tngd,knd->ngtk", queries, key_rows, preferred_element_type=jnp.float32)
        * score_scale
    )
    weights = jnp.where(allowed[None, None], jnp.exp(scores), 0.0)
    probs = weights / jnp.sum(weights, axis=-1, keepdims=True)
    probs_low = probs.astype(jnp.bfloat16)
    attended = jnp.einsum("ngtk,knd->tngd", probs_low, values, preferred_element_type=jnp.float32)
    dprobs = jnp.einsum("tngd,knd->ngtk", upstream, values, preferred_element_type=jnp.float32)
    delta = jnp.sum(probs * dprobs, axis=-1, keepdims=True)
    dscores = (probs * (dprobs - delta) * score_scale).astype(jnp.bfloat16)
    dqueries = jnp.einsum("ngtk,knd->tngd", dscores, key_rows, preferred_element_type=jnp.float32)
    return (attended.astype(jnp.bfloat16), dqueries)


def local(
    tokens,
    w_query,
    w_key,
    w_value,
    query_gain,
    key_gain,
    adapter_down,
    adapter_up,
    adapter_ids,
    doc_ids,
    cotangent,
):
    tok_count = tokens.shape[0]
    feat_width = tokens.shape[1]
    q_width = w_query.shape[1]
    kv_width = w_key.shape[1]
    local_heads = q_width // HD
    kv_heads = kv_width // HD
    head_group = local_heads // kv_heads
    positions = lax.axis_index("seq") * tok_count + jnp.arange(tok_count, dtype=jnp.int32)
    shard_cols = lax.all_gather(tokens, "tensor", axis=1, tiled=True)
    query_lin = jnp.dot(shard_cols, w_query, preferred_element_type=jnp.float32)
    key_lin = jnp.dot(shard_cols, w_key, preferred_element_type=jnp.float32)
    value_lin = jnp.dot(shard_cols, w_value, preferred_element_type=jnp.float32)
    token_adapter = adapter_ids[:, 0]
    chosen = token_adapter[:, None] == jnp.arange(ADAPTERS, dtype=jnp.int32)[None, :]
    before = jnp.cumsum(chosen.astype(jnp.int32), axis=0) - 1
    slot_rank = jnp.sum(jnp.where(chosen, before, 0), axis=1)
    slot_index = token_adapter * CAP + slot_rank
    dispatch = (slot_index[None, :] == jnp.arange(ADAPTERS * CAP, dtype=jnp.int32)[:, None]).astype(
        jnp.bfloat16
    )
    outgoing = jnp.dot(dispatch, tokens, preferred_element_type=jnp.float32).astype(jnp.bfloat16)
    seq_count = lax.axis_size("seq")
    tensor_count = lax.axis_size("tensor")
    part = CAP // tensor_count
    both = ("seq", "tensor")
    down_full = lax.all_gather(adapter_down, "tensor", axis=2, tiled=True)[0].reshape(
        R, tensor_count, feat_width
    )
    up_full = lax.all_gather(adapter_up, "tensor", axis=2, tiled=True)[0].reshape(
        R, tensor_count, q_width
    )
    arrived = lax.all_to_all(outgoing, both, 0, 0, tiled=True).reshape(
        seq_count, tensor_count, part, feat_width
    )
    slot_low = jnp.einsum(
        "stkf,rtf->skr", arrived, down_full, preferred_element_type=jnp.float32
    ).astype(jnp.bfloat16)
    slot_lift = jnp.einsum(
        "skr,rte->stke", slot_low, up_full, preferred_element_type=jnp.float32
    ).astype(jnp.bfloat16)
    back_lift = lax.all_to_all(
        slot_lift.reshape(seq_count * tensor_count * part, q_width), both, 0, 0, tiled=True
    )
    lifted = jnp.einsum(
        "st,se->te",
        dispatch,
        back_lift,
        preferred_element_type=jnp.float32,
    ).astype(jnp.bfloat16)
    query_pre = (query_lin + lifted.astype(jnp.float32)).reshape(tok_count, local_heads, HD)
    queries, query_back = jax.vjp(
        lambda pre_query: shape_query(pre_query, query_gain, positions), query_pre
    )
    queries = queries.astype(jnp.bfloat16).reshape(tok_count, kv_heads, head_group, HD)
    key_rows = shape_query(key_lin.reshape(tok_count, kv_heads, HD), key_gain, positions).astype(
        jnp.bfloat16
    )
    values = value_lin.astype(jnp.bfloat16).reshape(tok_count, kv_heads, HD)
    rim_count = WINDOW // tok_count
    key_list = []
    value_list = []
    doc_list = []
    place_list = []
    for distance in range(rim_count, 0, -1):
        far_keys, far_values, far_docs = passed_along((key_rows, values, doc_ids), "seq", distance)
        key_list.append(far_keys)
        value_list.append(far_values)
        doc_list.append(far_docs)
        place_list.append(positions - distance * tok_count)
    key_list.append(key_rows)
    value_list.append(values)
    doc_list.append(doc_ids)
    place_list.append(positions)
    window_keys = jnp.concatenate(key_list, axis=0)
    window_values = jnp.concatenate(value_list, axis=0)
    key_docs = jnp.concatenate(doc_list, axis=0)
    key_pos = jnp.concatenate(place_list, axis=0)
    key_gap = positions[:, None] - key_pos[None, :]
    allowed = (
        (doc_ids[:, None] == key_docs[None, :])
        & (key_gap >= 0)
        & (key_gap < WINDOW)
        & (key_pos[None, :] >= 0)
    )
    upstream = cotangent.reshape(tok_count, kv_heads, head_group, HD)
    block_out, dqueries = attend(queries, window_keys, window_values, upstream, allowed)
    attended = block_out.reshape(tok_count, q_width)
    (dquery_pre,) = query_back(dqueries.reshape(tok_count, local_heads, HD))
    dquery_pre = dquery_pre.reshape(tok_count, q_width).astype(jnp.bfloat16)
    out_grad = jnp.dot(dispatch, dquery_pre, preferred_element_type=jnp.float32).astype(
        jnp.bfloat16
    )
    low_rows = lax.all_gather(slot_low, "tensor", axis=0)
    grad_rows = lax.all_to_all(out_grad, "seq", 0, 0, tiled=True).reshape(
        seq_count, tensor_count, part, q_width
    )
    grad_up = jnp.einsum(
        "tskr,stke->re", low_rows, grad_rows, preferred_element_type=jnp.float32
    )[None]
    return (attended, grad_up)


def solution(mesh):
    in_specs = (
        P("seq", "tensor"),
        P(None, "tensor"),
        P(None, "tensor"),
        P(None, "tensor"),
        P(),
        P(),
        P("seq", None, "tensor"),
        P("seq", None, "tensor"),
        P("seq", None),
        P("seq"),
        P("seq", "tensor"),
    )
    out_specs = (P("seq", "tensor"), P("seq", None, "tensor"))
    return jax.shard_map(local, mesh=mesh, in_specs=in_specs, out_specs=out_specs, check_vma=False)
```

```python
import math

import jax
import jax.numpy as jnp
from jax import lax
from jax.sharding import Mesh, PartitionSpec as P

HD = 256
R = 64
WINDOW = 1024
ADAPTERS = 64
CAP = 16
SEQ = ("sy", "szc")


def passed_along(value, axis, steps):
    count = lax.axis_size(axis)
    first, last = (max(0, -steps), min(count, count - steps))
    return lax.ppermute(value, axis, [(source, source + steps) for source in range(first, last)])


def normalize(pre_field, gain_vec):
    mean_sq = jnp.mean(pre_field * pre_field, axis=-1, keepdims=True)
    return pre_field * lax.rsqrt(mean_sq + 1e-06) * gain_vec


def rotate(pre_field, positions):
    half_dim = pre_field.shape[-1] // 2
    frequency = jnp.exp(
        jnp.arange(half_dim, dtype=jnp.float32) * (-2.0 * math.log(10000.0) / pre_field.shape[-1])
    )
    angles = positions.astype(jnp.float32)[:, None] * frequency[None, :]
    cosine = jnp.cos(angles)[:, None, :]
    sine_part = jnp.sin(angles)[:, None, :]
    lower_half = pre_field[..., :half_dim]
    second = pre_field[..., half_dim:]
    return jnp.concatenate(
        [lower_half * cosine - second * sine_part, second * cosine + lower_half * sine_part],
        axis=-1,
    )


def shape_query(pre_field, gain_vec, positions):
    return rotate(normalize(pre_field, gain_vec), positions)


def attend(queries, key_rows, values, upstream, allowed):
    score_scale = 1.0 / math.sqrt(queries.shape[-1])
    scores = (
        jnp.einsum("tngd,knd->ngtk", queries, key_rows, preferred_element_type=jnp.float32)
        * score_scale
    )
    weights = jnp.where(allowed[None, None], jnp.exp(scores), 0.0)
    probs = weights / jnp.sum(weights, axis=-1, keepdims=True)
    probs_low = probs.astype(jnp.bfloat16)
    attended = jnp.einsum("ngtk,knd->tngd", probs_low, values, preferred_element_type=jnp.float32)
    dprobs = jnp.einsum("tngd,knd->ngtk", upstream, values, preferred_element_type=jnp.float32)
    delta = jnp.sum(probs * dprobs, axis=-1, keepdims=True)
    dscores = (probs * (dprobs - delta) * score_scale).astype(jnp.bfloat16)
    dqueries = jnp.einsum("ngtk,knd->tngd", dscores, key_rows, preferred_element_type=jnp.float32)
    return (attended.astype(jnp.bfloat16), dqueries)


def local(
    tokens,
    w_query,
    w_key,
    w_value,
    query_gain,
    key_gain,
    adapter_down,
    adapter_up,
    adapter_ids,
    doc_ids,
    cotangent,
):
    tok_count = tokens.shape[0]
    feat_width = tokens.shape[1]
    q_width = w_query.shape[1]
    kv_width = w_key.shape[1]
    local_heads = q_width // HD
    kv_heads = kv_width // HD
    head_group = local_heads // kv_heads
    zc_count = lax.axis_size("szc")
    y_count = lax.axis_size("sy")
    seq_index = lax.axis_index("sy") * zc_count + lax.axis_index("szc")
    positions = seq_index * tok_count + jnp.arange(tok_count, dtype=jnp.int32)
    shard_cols = lax.all_gather(tokens, "tensor", axis=1, tiled=True)
    query_lin = jnp.dot(shard_cols, w_query, preferred_element_type=jnp.float32)
    key_lin = jnp.dot(shard_cols, w_key, preferred_element_type=jnp.float32)
    value_lin = jnp.dot(shard_cols, w_value, preferred_element_type=jnp.float32)
    token_adapter = adapter_ids[:, 0]
    chosen = token_adapter[:, None] == jnp.arange(ADAPTERS, dtype=jnp.int32)[None, :]
    before = jnp.cumsum(chosen.astype(jnp.int32), axis=0) - 1
    slot_rank = jnp.sum(jnp.where(chosen, before, 0), axis=1)
    slot_index = ((token_adapter % zc_count) * y_count + token_adapter // zc_count) * CAP + slot_rank
    dispatch = (slot_index[None, :] == jnp.arange(ADAPTERS * CAP, dtype=jnp.int32)[:, None]).astype(
        jnp.bfloat16
    )
    outgoing = jnp.dot(dispatch, tokens, preferred_element_type=jnp.float32).astype(jnp.bfloat16)
    column_down = lax.all_gather(adapter_down[0], "sy", axis=0)
    column_up = lax.all_gather(adapter_up[0], "sy", axis=0)
    arrived = lax.all_to_all(outgoing, "szc", 0, 0, tiled=True).reshape(
        zc_count, y_count, CAP, feat_width
    )
    partial_low = jnp.einsum(
        "sycd,yrd->sycr", arrived, column_down, preferred_element_type=jnp.float32
    )
    slot_low = lax.psum(partial_low, "tensor").astype(jnp.bfloat16)
    slot_lift = jnp.einsum(
        "sycr,yre->syce", slot_low, column_up, preferred_element_type=jnp.float32
    ).astype(jnp.bfloat16)
    back_lift = lax.all_to_all(
        slot_lift.reshape(zc_count * y_count * CAP, q_width), "szc", 0, 0, tiled=True
    )
    lifted = jnp.einsum(
        "st,se->te",
        dispatch,
        back_lift,
        preferred_element_type=jnp.float32,
    ).astype(jnp.bfloat16)
    query_pre = (query_lin + lifted.astype(jnp.float32)).reshape(tok_count, local_heads, HD)
    queries, query_back = jax.vjp(
        lambda pre_query: shape_query(pre_query, query_gain, positions), query_pre
    )
    queries = queries.astype(jnp.bfloat16).reshape(tok_count, kv_heads, head_group, HD)
    key_rows = shape_query(key_lin.reshape(tok_count, kv_heads, HD), key_gain, positions).astype(
        jnp.bfloat16
    )
    values = value_lin.astype(jnp.bfloat16).reshape(tok_count, kv_heads, HD)
    rim_count = WINDOW // tok_count
    key_list = []
    value_list = []
    doc_list = []
    place_list = []
    for distance in range(rim_count, 0, -1):
        far_keys, far_values, far_docs = passed_along((key_rows, values, doc_ids), SEQ, distance)
        key_list.append(far_keys)
        value_list.append(far_values)
        doc_list.append(far_docs)
        place_list.append(positions - distance * tok_count)
    key_list.append(key_rows)
    value_list.append(values)
    doc_list.append(doc_ids)
    place_list.append(positions)
    window_keys = jnp.concatenate(key_list, axis=0)
    window_values = jnp.concatenate(value_list, axis=0)
    key_docs = jnp.concatenate(doc_list, axis=0)
    key_pos = jnp.concatenate(place_list, axis=0)
    key_gap = positions[:, None] - key_pos[None, :]
    allowed = (
        (doc_ids[:, None] == key_docs[None, :])
        & (key_gap >= 0)
        & (key_gap < WINDOW)
        & (key_pos[None, :] >= 0)
    )
    upstream = cotangent.reshape(tok_count, kv_heads, head_group, HD)
    block_out, dqueries = attend(queries, window_keys, window_values, upstream, allowed)
    attended = block_out.reshape(tok_count, q_width)
    (dquery_pre,) = query_back(dqueries.reshape(tok_count, local_heads, HD))
    dquery_pre = dquery_pre.reshape(tok_count, q_width).astype(jnp.bfloat16)
    out_grad = jnp.dot(dispatch, dquery_pre, preferred_element_type=jnp.float32).astype(
        jnp.bfloat16
    )
    grad_rows = lax.all_to_all(out_grad, "szc", 0, 0, tiled=True).reshape(
        zc_count, y_count, CAP, q_width
    )
    column_grad = jnp.einsum(
        "sycr,syce->yre", slot_low, grad_rows, preferred_element_type=jnp.float32
    )
    grad_up = lax.psum_scatter(column_grad, "sy", scatter_dimension=0, tiled=True)
    return (attended, grad_up)


def solution(mesh):
    seq_size = mesh.shape["seq"]
    zc_size = seq_size // 4
    fine = Mesh(
        mesh.devices.reshape(4, zc_size, mesh.shape["tensor"]), ("sy", "szc", "tensor")
    )
    in_specs = (
        P(SEQ, "tensor"),
        P(None, "tensor"),
        P(None, "tensor"),
        P(None, "tensor"),
        P(),
        P(),
        P(SEQ, None, "tensor"),
        P(SEQ, None, "tensor"),
        P(SEQ, None),
        P(SEQ),
        P(SEQ, "tensor"),
    )
    out_specs = (P(SEQ, "tensor"), P(SEQ, None, "tensor"))
    return jax.shard_map(local, mesh=fine, in_specs=in_specs, out_specs=out_specs, check_vma=False)
```

```python
import math

import jax
import jax.numpy as jnp
from jax import lax
from jax.sharding import PartitionSpec as P

HD = 256
R = 64
WINDOW = 1024
ADAPTERS = 64
CAP = 16


def passed_along(value, axis, steps):
    count = lax.axis_size(axis)
    first, last = (max(0, -steps), min(count, count - steps))
    return lax.ppermute(value, axis, [(source, source + steps) for source in range(first, last)])


def normalize(pre_field, gain_vec):
    mean_sq = jnp.mean(pre_field * pre_field, axis=-1, keepdims=True)
    return pre_field * lax.rsqrt(mean_sq + 1e-06) * gain_vec


def rotate(pre_field, positions):
    half_dim = pre_field.shape[-1] // 2
    frequency = jnp.exp(
        jnp.arange(half_dim, dtype=jnp.float32) * (-2.0 * math.log(10000.0) / pre_field.shape[-1])
    )
    angles = positions.astype(jnp.float32)[:, None] * frequency[None, :]
    cosine = jnp.cos(angles)[:, None, :]
    sine_part = jnp.sin(angles)[:, None, :]
    lower_half = pre_field[..., :half_dim]
    second = pre_field[..., half_dim:]
    return jnp.concatenate(
        [lower_half * cosine - second * sine_part, second * cosine + lower_half * sine_part],
        axis=-1,
    )


def shape_query(pre_field, gain_vec, positions):
    return rotate(normalize(pre_field, gain_vec), positions)


def attend(queries, key_rows, values, upstream, allowed):
    score_scale = 1.0 / math.sqrt(queries.shape[-1])
    scores = (
        jnp.einsum("tngd,knd->ngtk", queries, key_rows, preferred_element_type=jnp.float32)
        * score_scale
    )
    weights = jnp.where(allowed[None, None], jnp.exp(scores), 0.0)
    probs = weights / jnp.sum(weights, axis=-1, keepdims=True)
    probs_low = probs.astype(jnp.bfloat16)
    attended = jnp.einsum("ngtk,knd->tngd", probs_low, values, preferred_element_type=jnp.float32)
    dprobs = jnp.einsum("tngd,knd->ngtk", upstream, values, preferred_element_type=jnp.float32)
    delta = jnp.sum(probs * dprobs, axis=-1, keepdims=True)
    dscores = (probs * (dprobs - delta) * score_scale).astype(jnp.bfloat16)
    dqueries = jnp.einsum("ngtk,knd->tngd", dscores, key_rows, preferred_element_type=jnp.float32)
    return (attended.astype(jnp.bfloat16), dqueries)


def local(
    tokens,
    w_query,
    w_key,
    w_value,
    query_gain,
    key_gain,
    adapter_down,
    adapter_up,
    adapter_ids,
    doc_ids,
    cotangent,
):
    tok_count = tokens.shape[0]
    feat_width = tokens.shape[1]
    q_width = w_query.shape[1]
    kv_width = w_key.shape[1]
    local_heads = q_width // HD
    kv_heads = kv_width // HD
    head_group = local_heads // kv_heads
    positions = lax.axis_index("seq") * tok_count + jnp.arange(tok_count, dtype=jnp.int32)
    shard_cols = lax.all_gather(tokens, "tensor", axis=1, tiled=True)
    query_lin = jnp.dot(shard_cols, w_query, preferred_element_type=jnp.float32)
    key_lin = jnp.dot(shard_cols, w_key, preferred_element_type=jnp.float32)
    value_lin = jnp.dot(shard_cols, w_value, preferred_element_type=jnp.float32)
    token_adapter = adapter_ids[:, 0]
    chosen = token_adapter[:, None] == jnp.arange(ADAPTERS, dtype=jnp.int32)[None, :]
    before = jnp.cumsum(chosen.astype(jnp.int32), axis=0) - 1
    slot_rank = jnp.sum(jnp.where(chosen, before, 0), axis=1)
    slot_index = token_adapter * CAP + slot_rank
    dispatch = (slot_index[None, :] == jnp.arange(ADAPTERS * CAP, dtype=jnp.int32)[:, None]).astype(
        jnp.bfloat16
    )
    outgoing = jnp.dot(dispatch, tokens, preferred_element_type=jnp.float32).astype(jnp.bfloat16)
    seq_count = lax.axis_size("seq")
    own_adapters = adapter_down.shape[0]
    arrived = lax.all_to_all(outgoing, "seq", 0, 0, tiled=True).reshape(
        seq_count, own_adapters, CAP, feat_width
    )
    partial_low = jnp.einsum(
        "sacd,ard->sacr", arrived, adapter_down, preferred_element_type=jnp.float32
    )
    slot_low = lax.psum(partial_low, "tensor").astype(jnp.bfloat16)
    all_up = lax.all_gather(adapter_up, "seq", axis=0, tiled=True)
    back_low = lax.all_to_all(
        slot_low.reshape(seq_count * own_adapters * CAP, R), "seq", 0, 0, tiled=True
    ).reshape(ADAPTERS, CAP, R)
    slot_lift = jnp.einsum(
        "acr,are->ace", back_low, all_up, preferred_element_type=jnp.float32
    ).astype(jnp.bfloat16)
    lifted = jnp.einsum(
        "st,se->te",
        dispatch,
        slot_lift.reshape(ADAPTERS * CAP, q_width),
        preferred_element_type=jnp.float32,
    ).astype(jnp.bfloat16)
    query_pre = (query_lin + lifted.astype(jnp.float32)).reshape(tok_count, local_heads, HD)
    queries, query_back = jax.vjp(
        lambda pre_query: shape_query(pre_query, query_gain, positions), query_pre
    )
    queries = queries.astype(jnp.bfloat16).reshape(tok_count, kv_heads, head_group, HD)
    key_rows = shape_query(key_lin.reshape(tok_count, kv_heads, HD), key_gain, positions).astype(
        jnp.bfloat16
    )
    values = value_lin.astype(jnp.bfloat16).reshape(tok_count, kv_heads, HD)
    rim_count = WINDOW // tok_count
    key_list = []
    value_list = []
    doc_list = []
    place_list = []
    for distance in range(rim_count, 0, -1):
        far_keys, far_values, far_docs = passed_along((key_rows, values, doc_ids), "seq", distance)
        key_list.append(far_keys)
        value_list.append(far_values)
        doc_list.append(far_docs)
        place_list.append(positions - distance * tok_count)
    key_list.append(key_rows)
    value_list.append(values)
    doc_list.append(doc_ids)
    place_list.append(positions)
    window_keys = jnp.concatenate(key_list, axis=0)
    window_values = jnp.concatenate(value_list, axis=0)
    key_docs = jnp.concatenate(doc_list, axis=0)
    key_pos = jnp.concatenate(place_list, axis=0)
    key_gap = positions[:, None] - key_pos[None, :]
    allowed = (
        (doc_ids[:, None] == key_docs[None, :])
        & (key_gap >= 0)
        & (key_gap < WINDOW)
        & (key_pos[None, :] >= 0)
    )
    upstream = cotangent.reshape(tok_count, kv_heads, head_group, HD)
    block_out, dqueries = attend(queries, window_keys, window_values, upstream, allowed)
    attended = block_out.reshape(tok_count, q_width)
    (dquery_pre,) = query_back(dqueries.reshape(tok_count, local_heads, HD))
    dquery_pre = dquery_pre.reshape(tok_count, q_width).astype(jnp.bfloat16)
    out_grad = jnp.dot(dispatch, dquery_pre, preferred_element_type=jnp.float32).astype(
        jnp.bfloat16
    )
    grad_rows = lax.all_to_all(out_grad, "seq", 0, 0, tiled=True).reshape(
        seq_count, own_adapters, CAP, q_width
    )
    grad_up = jnp.einsum(
        "sacr,sace->are", slot_low, grad_rows, preferred_element_type=jnp.float32
    )
    return (attended, grad_up)


def solution(mesh):
    in_specs = (
        P("seq", "tensor"),
        P(None, "tensor"),
        P(None, "tensor"),
        P(None, "tensor"),
        P(),
        P(),
        P("seq", None, "tensor"),
        P("seq", None, "tensor"),
        P("seq", None),
        P("seq"),
        P("seq", "tensor"),
    )
    out_specs = (P("seq", "tensor"), P("seq", None, "tensor"))
    return jax.shard_map(local, mesh=mesh, in_specs=in_specs, out_specs=out_specs, check_vma=False)
```

```python
import math

import jax
import jax.numpy as jnp
from jax import lax
from jax.sharding import PartitionSpec as P

HD = 256
R = 64
WINDOW = 1024
ADAPTERS = 64
CAP = 16


def passed_along(value, axis, steps):
    count = lax.axis_size(axis)
    first, last = (max(0, -steps), min(count, count - steps))
    return lax.ppermute(value, axis, [(source, source + steps) for source in range(first, last)])


def normalize(pre_field, gain_vec):
    mean_sq = jnp.mean(pre_field * pre_field, axis=-1, keepdims=True)
    return pre_field * lax.rsqrt(mean_sq + 1e-06) * gain_vec


def rotate(pre_field, positions):
    half_dim = pre_field.shape[-1] // 2
    frequency = jnp.exp(
        jnp.arange(half_dim, dtype=jnp.float32) * (-2.0 * math.log(10000.0) / pre_field.shape[-1])
    )
    angles = positions.astype(jnp.float32)[:, None] * frequency[None, :]
    cosine = jnp.cos(angles)[:, None, :]
    sine_part = jnp.sin(angles)[:, None, :]
    lower_half = pre_field[..., :half_dim]
    second = pre_field[..., half_dim:]
    return jnp.concatenate(
        [lower_half * cosine - second * sine_part, second * cosine + lower_half * sine_part],
        axis=-1,
    )


def shape_query(pre_field, gain_vec, positions):
    return rotate(normalize(pre_field, gain_vec), positions)


def attend(queries, key_rows, values, upstream, allowed):
    score_scale = 1.0 / math.sqrt(queries.shape[-1])
    scores = (
        jnp.einsum("tngd,knd->ngtk", queries, key_rows, preferred_element_type=jnp.float32)
        * score_scale
    )
    weights = jnp.where(allowed[None, None], jnp.exp(scores), 0.0)
    probs = weights / jnp.sum(weights, axis=-1, keepdims=True)
    probs_low = probs.astype(jnp.bfloat16)
    attended = jnp.einsum("ngtk,knd->tngd", probs_low, values, preferred_element_type=jnp.float32)
    dprobs = jnp.einsum("tngd,knd->ngtk", upstream, values, preferred_element_type=jnp.float32)
    delta = jnp.sum(probs * dprobs, axis=-1, keepdims=True)
    dscores = (probs * (dprobs - delta) * score_scale).astype(jnp.bfloat16)
    dqueries = jnp.einsum("ngtk,knd->tngd", dscores, key_rows, preferred_element_type=jnp.float32)
    return (attended.astype(jnp.bfloat16), dqueries)


def local(
    tokens,
    w_query,
    w_key,
    w_value,
    query_gain,
    key_gain,
    adapter_down,
    adapter_up,
    adapter_ids,
    doc_ids,
    cotangent,
):
    tok_count = tokens.shape[0]
    feat_width = tokens.shape[1]
    q_width = w_query.shape[1]
    kv_width = w_key.shape[1]
    local_heads = q_width // HD
    kv_heads = kv_width // HD
    head_group = local_heads // kv_heads
    positions = lax.axis_index("seq") * tok_count + jnp.arange(tok_count, dtype=jnp.int32)
    shard_cols = lax.all_gather(tokens, "tensor", axis=1, tiled=True)
    query_lin = jnp.dot(shard_cols, w_query, preferred_element_type=jnp.float32)
    key_lin = jnp.dot(shard_cols, w_key, preferred_element_type=jnp.float32)
    value_lin = jnp.dot(shard_cols, w_value, preferred_element_type=jnp.float32)
    token_adapter = adapter_ids[:, 0]
    chosen = token_adapter[:, None] == jnp.arange(ADAPTERS, dtype=jnp.int32)[None, :]
    before = jnp.cumsum(chosen.astype(jnp.int32), axis=0) - 1
    slot_rank = jnp.sum(jnp.where(chosen, before, 0), axis=1)
    slot_index = token_adapter * CAP + slot_rank
    dispatch = (slot_index[None, :] == jnp.arange(ADAPTERS * CAP, dtype=jnp.int32)[:, None]).astype(
        jnp.bfloat16
    )
    outgoing = jnp.dot(dispatch, tokens, preferred_element_type=jnp.float32).astype(jnp.bfloat16)
    seq_count = lax.axis_size("seq")
    own_adapters = adapter_down.shape[0]
    arrived = lax.all_to_all(outgoing, "seq", 0, 0, tiled=True).reshape(
        seq_count, own_adapters, CAP, feat_width
    )
    key_rows = shape_query(key_lin.reshape(tok_count, kv_heads, HD), key_gain, positions).astype(
        jnp.bfloat16
    )
    values = value_lin.astype(jnp.bfloat16).reshape(tok_count, kv_heads, HD)
    rim_count = WINDOW // tok_count
    key_list = []
    value_list = []
    doc_list = []
    place_list = []
    for distance in range(rim_count, 0, -1):
        far_keys, far_values, far_docs = passed_along((key_rows, values, doc_ids), "seq", distance)
        key_list.append(far_keys)
        value_list.append(far_values)
        doc_list.append(far_docs)
        place_list.append(positions - distance * tok_count)
    key_list.append(key_rows)
    value_list.append(values)
    doc_list.append(doc_ids)
    place_list.append(positions)
    window_keys = jnp.concatenate(key_list, axis=0)
    window_values = jnp.concatenate(value_list, axis=0)
    key_docs = jnp.concatenate(doc_list, axis=0)
    key_pos = jnp.concatenate(place_list, axis=0)
    key_gap = positions[:, None] - key_pos[None, :]
    allowed = (
        (doc_ids[:, None] == key_docs[None, :])
        & (key_gap >= 0)
        & (key_gap < WINDOW)
        & (key_pos[None, :] >= 0)
    )
    arrived, query_lin, window_keys, window_values, allowed = lax.optimization_barrier(
        (arrived, query_lin, window_keys, window_values, allowed)
    )
    partial_low = jnp.einsum(
        "sacd,ard->sacr", arrived, adapter_down, preferred_element_type=jnp.float32
    )
    slot_low = lax.psum(partial_low, "tensor").astype(jnp.bfloat16)
    all_up = lax.all_gather(adapter_up, "seq", axis=0, tiled=True)
    back_low = lax.all_to_all(
        slot_low.reshape(seq_count * own_adapters * CAP, R), "seq", 0, 0, tiled=True
    ).reshape(ADAPTERS, CAP, R)
    slot_lift = jnp.einsum(
        "acr,are->ace", back_low, all_up, preferred_element_type=jnp.float32
    ).astype(jnp.bfloat16)
    lifted = jnp.einsum(
        "st,se->te",
        dispatch,
        slot_lift.reshape(ADAPTERS * CAP, q_width),
        preferred_element_type=jnp.float32,
    ).astype(jnp.bfloat16)
    query_pre = (query_lin + lifted.astype(jnp.float32)).reshape(tok_count, local_heads, HD)
    queries, query_back = jax.vjp(
        lambda pre_query: shape_query(pre_query, query_gain, positions), query_pre
    )
    queries = queries.astype(jnp.bfloat16).reshape(tok_count, kv_heads, head_group, HD)
    upstream = cotangent.reshape(tok_count, kv_heads, head_group, HD)
    block_out, dqueries = attend(queries, window_keys, window_values, upstream, allowed)
    attended = block_out.reshape(tok_count, q_width)
    (dquery_pre,) = query_back(dqueries.reshape(tok_count, local_heads, HD))
    dquery_pre = dquery_pre.reshape(tok_count, q_width).astype(jnp.bfloat16)
    out_grad = jnp.dot(dispatch, dquery_pre, preferred_element_type=jnp.float32).astype(
        jnp.bfloat16
    )
    grad_rows = lax.all_to_all(out_grad, "seq", 0, 0, tiled=True).reshape(
        seq_count, own_adapters, CAP, q_width
    )
    grad_up = jnp.einsum(
        "sacr,sace->are", slot_low, grad_rows, preferred_element_type=jnp.float32
    )
    return (attended, grad_up)


def solution(mesh):
    in_specs = (
        P("seq", "tensor"),
        P(None, "tensor"),
        P(None, "tensor"),
        P(None, "tensor"),
        P(),
        P(),
        P("seq", None, "tensor"),
        P("seq", None, "tensor"),
        P("seq", None),
        P("seq"),
        P("seq", "tensor"),
    )
    out_specs = (P("seq", "tensor"), P("seq", None, "tensor"))
    return jax.shard_map(local, mesh=mesh, in_specs=in_specs, out_specs=out_specs, check_vma=False)
```

```python
import math

import jax
import jax.numpy as jnp
from jax import lax
from jax.sharding import PartitionSpec as P

HD = 256
R = 64
WINDOW = 1024
ADAPTERS = 64
CAP = 16


def passed_along(value, axis, steps):
    count = lax.axis_size(axis)
    first, last = (max(0, -steps), min(count, count - steps))
    return lax.ppermute(value, axis, [(source, source + steps) for source in range(first, last)])


def normalize(pre_field, gain_vec):
    mean_sq = jnp.mean(pre_field * pre_field, axis=-1, keepdims=True)
    return pre_field * lax.rsqrt(mean_sq + 1e-06) * gain_vec


def rotate(pre_field, positions):
    half_dim = pre_field.shape[-1] // 2
    frequency = jnp.exp(
        jnp.arange(half_dim, dtype=jnp.float32) * (-2.0 * math.log(10000.0) / pre_field.shape[-1])
    )
    angles = positions.astype(jnp.float32)[:, None] * frequency[None, :]
    cosine = jnp.cos(angles)[:, None, :]
    sine_part = jnp.sin(angles)[:, None, :]
    lower_half = pre_field[..., :half_dim]
    second = pre_field[..., half_dim:]
    return jnp.concatenate(
        [lower_half * cosine - second * sine_part, second * cosine + lower_half * sine_part],
        axis=-1,
    )


def shape_query(pre_field, gain_vec, positions):
    return rotate(normalize(pre_field, gain_vec), positions)


def attend(queries, key_rows, values, upstream, allowed):
    score_scale = 1.0 / math.sqrt(queries.shape[-1])
    scores = (
        jnp.einsum("tngd,knd->ngtk", queries, key_rows, preferred_element_type=jnp.float32)
        * score_scale
    )
    weights = jnp.where(allowed[None, None], jnp.exp(scores), 0.0)
    probs = weights / jnp.sum(weights, axis=-1, keepdims=True)
    probs_low = probs.astype(jnp.bfloat16)
    attended = jnp.einsum("ngtk,knd->tngd", probs_low, values, preferred_element_type=jnp.float32)
    dprobs = jnp.einsum("tngd,knd->ngtk", upstream, values, preferred_element_type=jnp.float32)
    delta = jnp.sum(probs * dprobs, axis=-1, keepdims=True)
    dscores = (probs * (dprobs - delta) * score_scale).astype(jnp.bfloat16)
    dqueries = jnp.einsum("ngtk,knd->tngd", dscores, key_rows, preferred_element_type=jnp.float32)
    return (attended.astype(jnp.bfloat16), dqueries)


def local(
    tokens,
    w_query,
    w_key,
    w_value,
    query_gain,
    key_gain,
    adapter_down,
    adapter_up,
    adapter_ids,
    doc_ids,
    cotangent,
):
    tok_count = tokens.shape[0]
    feat_width = tokens.shape[1]
    q_width = w_query.shape[1]
    kv_width = w_key.shape[1]
    local_heads = q_width // HD
    kv_heads = kv_width // HD
    head_group = local_heads // kv_heads
    positions = lax.axis_index("seq") * tok_count + jnp.arange(tok_count, dtype=jnp.int32)
    shard_cols = lax.all_gather(tokens, "tensor", axis=1, tiled=True)
    query_lin = jnp.dot(shard_cols, w_query, preferred_element_type=jnp.float32)
    key_lin = jnp.dot(shard_cols, w_key, preferred_element_type=jnp.float32)
    value_lin = jnp.dot(shard_cols, w_value, preferred_element_type=jnp.float32)
    token_adapter = adapter_ids[:, 0]
    chosen = token_adapter[:, None] == jnp.arange(ADAPTERS, dtype=jnp.int32)[None, :]
    before = jnp.cumsum(chosen.astype(jnp.int32), axis=0) - 1
    slot_rank = jnp.sum(jnp.where(chosen, before, 0), axis=1)
    slot_index = token_adapter * CAP + slot_rank
    dispatch = (slot_index[None, :] == jnp.arange(ADAPTERS * CAP, dtype=jnp.int32)[:, None]).astype(
        jnp.bfloat16
    )
    outgoing = jnp.dot(dispatch, tokens, preferred_element_type=jnp.float32).astype(jnp.bfloat16)
    seq_count = lax.axis_size("seq")
    own_adapters = adapter_down.shape[0]
    arrived = lax.all_to_all(outgoing, "seq", 0, 0, tiled=True).reshape(
        seq_count, own_adapters, CAP, feat_width
    )
    key_rows = shape_query(key_lin.reshape(tok_count, kv_heads, HD), key_gain, positions).astype(
        jnp.bfloat16
    )
    values = value_lin.astype(jnp.bfloat16).reshape(tok_count, kv_heads, HD)
    rim_count = WINDOW // tok_count
    key_list = []
    value_list = []
    doc_list = []
    place_list = []
    kv_rows = jnp.stack([key_rows, values], axis=1)
    for distance in range(rim_count, 0, -1):
        far_kv, far_docs = passed_along((kv_rows, doc_ids), "seq", distance)
        key_list.append(far_kv[:, 0])
        value_list.append(far_kv[:, 1])
        doc_list.append(far_docs)
        place_list.append(positions - distance * tok_count)
    key_list.append(key_rows)
    value_list.append(values)
    doc_list.append(doc_ids)
    place_list.append(positions)
    window_keys = jnp.concatenate(key_list, axis=0)
    window_values = jnp.concatenate(value_list, axis=0)
    key_docs = jnp.concatenate(doc_list, axis=0)
    key_pos = jnp.concatenate(place_list, axis=0)
    key_gap = positions[:, None] - key_pos[None, :]
    allowed = (
        (doc_ids[:, None] == key_docs[None, :])
        & (key_gap >= 0)
        & (key_gap < WINDOW)
        & (key_pos[None, :] >= 0)
    )
    arrived, query_lin, window_keys, window_values, allowed = lax.optimization_barrier(
        (arrived, query_lin, window_keys, window_values, allowed)
    )
    partial_low = jnp.einsum(
        "sacd,ard->sacr", arrived, adapter_down, preferred_element_type=jnp.float32
    )
    slot_low = lax.psum(partial_low, "tensor").astype(jnp.bfloat16)
    all_up = lax.all_gather(adapter_up, "seq", axis=0, tiled=True)
    back_low = lax.all_to_all(
        slot_low.reshape(seq_count * own_adapters * CAP, R), "seq", 0, 0, tiled=True
    ).reshape(ADAPTERS, CAP, R)
    slot_lift = jnp.einsum(
        "acr,are->ace", back_low, all_up, preferred_element_type=jnp.float32
    ).astype(jnp.bfloat16)
    lifted = jnp.einsum(
        "st,se->te",
        dispatch,
        slot_lift.reshape(ADAPTERS * CAP, q_width),
        preferred_element_type=jnp.float32,
    ).astype(jnp.bfloat16)
    query_pre = (query_lin + lifted.astype(jnp.float32)).reshape(tok_count, local_heads, HD)
    queries, query_back = jax.vjp(
        lambda pre_query: shape_query(pre_query, query_gain, positions), query_pre
    )
    queries = queries.astype(jnp.bfloat16).reshape(tok_count, kv_heads, head_group, HD)
    upstream = cotangent.reshape(tok_count, kv_heads, head_group, HD)
    block_out, dqueries = attend(queries, window_keys, window_values, upstream, allowed)
    attended = block_out.reshape(tok_count, q_width)
    (dquery_pre,) = query_back(dqueries.reshape(tok_count, local_heads, HD))
    dquery_pre = dquery_pre.reshape(tok_count, q_width).astype(jnp.bfloat16)
    out_grad = jnp.dot(dispatch, dquery_pre, preferred_element_type=jnp.float32).astype(
        jnp.bfloat16
    )
    grad_rows = lax.all_to_all(out_grad, "seq", 0, 0, tiled=True).reshape(
        seq_count, own_adapters, CAP, q_width
    )
    grad_up = jnp.einsum(
        "sacr,sace->are", slot_low, grad_rows, preferred_element_type=jnp.float32
    )
    return (attended, grad_up)


def solution(mesh):
    in_specs = (
        P("seq", "tensor"),
        P(None, "tensor"),
        P(None, "tensor"),
        P(None, "tensor"),
        P(),
        P(),
        P("seq", None, "tensor"),
        P("seq", None, "tensor"),
        P("seq", None),
        P("seq"),
        P("seq", "tensor"),
    )
    out_specs = (P("seq", "tensor"), P("seq", None, "tensor"))
    return jax.shard_map(local, mesh=mesh, in_specs=in_specs, out_specs=out_specs, check_vma=False)
```

```python
import math

import jax
import jax.numpy as jnp
from jax import lax
from jax.sharding import PartitionSpec as P

HD = 256
R = 64
WINDOW = 1024
ADAPTERS = 64
CAP = 16


def passed_along(value, axis, steps):
    count = lax.axis_size(axis)
    first, last = (max(0, -steps), min(count, count - steps))
    return lax.ppermute(value, axis, [(source, source + steps) for source in range(first, last)])


def normalize(pre_field, gain_vec):
    mean_sq = jnp.mean(pre_field * pre_field, axis=-1, keepdims=True)
    return pre_field * lax.rsqrt(mean_sq + 1e-06) * gain_vec


def rotate(pre_field, positions):
    half_dim = pre_field.shape[-1] // 2
    frequency = jnp.exp(
        jnp.arange(half_dim, dtype=jnp.float32) * (-2.0 * math.log(10000.0) / pre_field.shape[-1])
    )
    angles = positions.astype(jnp.float32)[:, None] * frequency[None, :]
    cosine = jnp.cos(angles)[:, None, :]
    sine_part = jnp.sin(angles)[:, None, :]
    lower_half = pre_field[..., :half_dim]
    second = pre_field[..., half_dim:]
    return jnp.concatenate(
        [lower_half * cosine - second * sine_part, second * cosine + lower_half * sine_part],
        axis=-1,
    )


def shape_query(pre_field, gain_vec, positions):
    return rotate(normalize(pre_field, gain_vec), positions)


def attend(queries, key_rows, values, upstream, allowed):
    score_scale = 1.0 / math.sqrt(queries.shape[-1])
    scores = (
        jnp.einsum("tngd,knd->ngtk", queries, key_rows, preferred_element_type=jnp.float32)
        * score_scale
    )
    weights = jnp.where(allowed[None, None], jnp.exp(scores), 0.0)
    probs = weights / jnp.sum(weights, axis=-1, keepdims=True)
    probs_low = probs.astype(jnp.bfloat16)
    attended = jnp.einsum("ngtk,knd->tngd", probs_low, values, preferred_element_type=jnp.float32)
    dprobs = jnp.einsum("tngd,knd->ngtk", upstream, values, preferred_element_type=jnp.float32)
    delta = jnp.sum(probs * dprobs, axis=-1, keepdims=True)
    dscores = (probs * (dprobs - delta) * score_scale).astype(jnp.bfloat16)
    dqueries = jnp.einsum("ngtk,knd->tngd", dscores, key_rows, preferred_element_type=jnp.float32)
    return (attended.astype(jnp.bfloat16), dqueries)


def local(
    tokens,
    w_query,
    w_key,
    w_value,
    query_gain,
    key_gain,
    adapter_down,
    adapter_up,
    adapter_ids,
    doc_ids,
    cotangent,
):
    tok_count = tokens.shape[0]
    feat_width = tokens.shape[1]
    q_width = w_query.shape[1]
    kv_width = w_key.shape[1]
    local_heads = q_width // HD
    kv_heads = kv_width // HD
    head_group = local_heads // kv_heads
    positions = lax.axis_index("seq") * tok_count + jnp.arange(tok_count, dtype=jnp.int32)
    shard_cols = lax.all_gather(tokens, "tensor", axis=1, tiled=True)
    query_lin = jnp.dot(shard_cols, w_query, preferred_element_type=jnp.float32)
    key_lin = jnp.dot(shard_cols, w_key, preferred_element_type=jnp.float32)
    value_lin = jnp.dot(shard_cols, w_value, preferred_element_type=jnp.float32)
    token_adapter = adapter_ids[:, 0]
    chosen = token_adapter[:, None] == jnp.arange(ADAPTERS, dtype=jnp.int32)[None, :]
    before = jnp.cumsum(chosen.astype(jnp.int32), axis=0) - 1
    slot_rank = jnp.sum(jnp.where(chosen, before, 0), axis=1)
    slot_index = token_adapter * CAP + slot_rank
    dispatch = (slot_index[None, :] == jnp.arange(ADAPTERS * CAP, dtype=jnp.int32)[:, None]).astype(
        jnp.bfloat16
    )
    outgoing = jnp.dot(dispatch, tokens, preferred_element_type=jnp.float32).astype(jnp.bfloat16)
    seq_count = lax.axis_size("seq")
    own_adapters = adapter_down.shape[0]
    arrived = lax.all_to_all(outgoing, "seq", 0, 0, tiled=True).reshape(
        seq_count, own_adapters, CAP, feat_width
    )
    key_rows = shape_query(key_lin.reshape(tok_count, kv_heads, HD), key_gain, positions).astype(
        jnp.bfloat16
    )
    values = value_lin.astype(jnp.bfloat16).reshape(tok_count, kv_heads, HD)
    rim_count = WINDOW // tok_count
    doc_list = []
    place_list = []
    for distance in range(rim_count, 0, -1):
        doc_list.append(passed_along(doc_ids, "seq", distance))
        place_list.append(positions - distance * tok_count)
    doc_list.append(doc_ids)
    place_list.append(positions)
    key_docs = jnp.concatenate(doc_list, axis=0)
    key_pos = jnp.concatenate(place_list, axis=0)
    key_gap = positions[:, None] - key_pos[None, :]
    allowed = (
        (doc_ids[:, None] == key_docs[None, :])
        & (key_gap >= 0)
        & (key_gap < WINDOW)
        & (key_pos[None, :] >= 0)
    )
    kv_rows = jnp.stack([key_rows, values], axis=1)
    arrived, query_lin, kv_rows, allowed = lax.optimization_barrier(
        (arrived, query_lin, kv_rows, allowed)
    )
    key_list = []
    value_list = []
    for distance in range(rim_count, 0, -1):
        far_kv = passed_along(kv_rows, "seq", distance)
        key_list.append(far_kv[:, 0])
        value_list.append(far_kv[:, 1])
    key_list.append(kv_rows[:, 0])
    value_list.append(kv_rows[:, 1])
    window_keys = jnp.concatenate(key_list, axis=0)
    window_values = jnp.concatenate(value_list, axis=0)
    partial_low = jnp.einsum(
        "sacd,ard->sacr", arrived, adapter_down, preferred_element_type=jnp.float32
    )
    slot_low = lax.psum(partial_low, "tensor").astype(jnp.bfloat16)
    all_up = lax.all_gather(adapter_up, "seq", axis=0, tiled=True)
    back_low = lax.all_to_all(
        slot_low.reshape(seq_count * own_adapters * CAP, R), "seq", 0, 0, tiled=True
    ).reshape(ADAPTERS, CAP, R)
    slot_lift = jnp.einsum(
        "acr,are->ace", back_low, all_up, preferred_element_type=jnp.float32
    ).astype(jnp.bfloat16)
    lifted = jnp.einsum(
        "st,se->te",
        dispatch,
        slot_lift.reshape(ADAPTERS * CAP, q_width),
        preferred_element_type=jnp.float32,
    ).astype(jnp.bfloat16)
    query_pre = (query_lin + lifted.astype(jnp.float32)).reshape(tok_count, local_heads, HD)
    queries, query_back = jax.vjp(
        lambda pre_query: shape_query(pre_query, query_gain, positions), query_pre
    )
    queries = queries.astype(jnp.bfloat16).reshape(tok_count, kv_heads, head_group, HD)
    upstream = cotangent.reshape(tok_count, kv_heads, head_group, HD)
    block_out, dqueries = attend(queries, window_keys, window_values, upstream, allowed)
    attended = block_out.reshape(tok_count, q_width)
    (dquery_pre,) = query_back(dqueries.reshape(tok_count, local_heads, HD))
    dquery_pre = dquery_pre.reshape(tok_count, q_width).astype(jnp.bfloat16)
    out_grad = jnp.dot(dispatch, dquery_pre, preferred_element_type=jnp.float32).astype(
        jnp.bfloat16
    )
    grad_rows = lax.all_to_all(out_grad, "seq", 0, 0, tiled=True).reshape(
        seq_count, own_adapters, CAP, q_width
    )
    grad_up = jnp.einsum(
        "sacr,sace->are", slot_low, grad_rows, preferred_element_type=jnp.float32
    )
    return (attended, grad_up)


def solution(mesh):
    in_specs = (
        P("seq", "tensor"),
        P(None, "tensor"),
        P(None, "tensor"),
        P(None, "tensor"),
        P(),
        P(),
        P("seq", None, "tensor"),
        P("seq", None, "tensor"),
        P("seq", None),
        P("seq"),
        P("seq", "tensor"),
    )
    out_specs = (P("seq", "tensor"), P("seq", None, "tensor"))
    return jax.shard_map(local, mesh=mesh, in_specs=in_specs, out_specs=out_specs, check_vma=False)
```

```python
import math

import jax
import jax.numpy as jnp
from jax import lax
from jax.sharding import PartitionSpec as P

HD = 256
R = 64
WINDOW = 1024
ADAPTERS = 64
CAP = 16


def passed_along(value, axis, steps):
    count = lax.axis_size(axis)
    first, last = (max(0, -steps), min(count, count - steps))
    return lax.ppermute(value, axis, [(source, source + steps) for source in range(first, last)])


def normalize(pre_field, gain_vec):
    mean_sq = jnp.mean(pre_field * pre_field, axis=-1, keepdims=True)
    return pre_field * lax.rsqrt(mean_sq + 1e-06) * gain_vec


def rotate(pre_field, positions):
    half_dim = pre_field.shape[-1] // 2
    frequency = jnp.exp(
        jnp.arange(half_dim, dtype=jnp.float32) * (-2.0 * math.log(10000.0) / pre_field.shape[-1])
    )
    angles = positions.astype(jnp.float32)[:, None] * frequency[None, :]
    cosine = jnp.cos(angles)[:, None, :]
    sine_part = jnp.sin(angles)[:, None, :]
    lower_half = pre_field[..., :half_dim]
    second = pre_field[..., half_dim:]
    return jnp.concatenate(
        [lower_half * cosine - second * sine_part, second * cosine + lower_half * sine_part],
        axis=-1,
    )


def shape_query(pre_field, gain_vec, positions):
    return rotate(normalize(pre_field, gain_vec), positions)


def attend(queries, key_rows, values, upstream, allowed):
    score_scale = 1.0 / math.sqrt(queries.shape[-1])
    scores = (
        jnp.einsum("tngd,knd->ngtk", queries, key_rows, preferred_element_type=jnp.float32)
        * score_scale
    )
    weights = jnp.where(allowed[None, None], jnp.exp(scores), 0.0)
    probs = weights / jnp.sum(weights, axis=-1, keepdims=True)
    probs_low = probs.astype(jnp.bfloat16)
    attended = jnp.einsum("ngtk,knd->tngd", probs_low, values, preferred_element_type=jnp.float32)
    dprobs = jnp.einsum("tngd,knd->ngtk", upstream, values, preferred_element_type=jnp.float32)
    delta = jnp.sum(probs * dprobs, axis=-1, keepdims=True)
    dscores = (probs * (dprobs - delta) * score_scale).astype(jnp.bfloat16)
    dqueries = jnp.einsum("ngtk,knd->tngd", dscores, key_rows, preferred_element_type=jnp.float32)
    return (attended.astype(jnp.bfloat16), dqueries)


def local(
    tokens,
    w_query,
    w_key,
    w_value,
    query_gain,
    key_gain,
    adapter_down,
    adapter_up,
    adapter_ids,
    doc_ids,
    cotangent,
):
    tok_count = tokens.shape[0]
    feat_width = tokens.shape[1]
    q_width = w_query.shape[1]
    kv_width = w_key.shape[1]
    local_heads = q_width // HD
    kv_heads = kv_width // HD
    head_group = local_heads // kv_heads
    positions = lax.axis_index("seq") * tok_count + jnp.arange(tok_count, dtype=jnp.int32)
    shard_cols = lax.all_gather(tokens, "tensor", axis=1, tiled=True)
    query_lin = jnp.dot(shard_cols, w_query, preferred_element_type=jnp.float32)
    key_lin = jnp.dot(shard_cols, w_key, preferred_element_type=jnp.float32)
    value_lin = jnp.dot(shard_cols, w_value, preferred_element_type=jnp.float32)
    token_adapter = adapter_ids[:, 0]
    chosen = token_adapter[:, None] == jnp.arange(ADAPTERS, dtype=jnp.int32)[None, :]
    before = jnp.cumsum(chosen.astype(jnp.int32), axis=0) - 1
    slot_rank = jnp.sum(jnp.where(chosen, before, 0), axis=1)
    slot_index = token_adapter * CAP + slot_rank
    dispatch = (slot_index[None, :] == jnp.arange(ADAPTERS * CAP, dtype=jnp.int32)[:, None]).astype(
        jnp.bfloat16
    )
    dispatch_t = (slot_index[:, None] == jnp.arange(ADAPTERS * CAP, dtype=jnp.int32)[None, :]).astype(
        jnp.bfloat16
    )
    outgoing = jnp.einsum(
        "ts,td->sd", dispatch_t, tokens, preferred_element_type=jnp.bfloat16
    )
    seq_count = lax.axis_size("seq")
    own_adapters = adapter_down.shape[0]
    arrived = lax.all_to_all(outgoing, "seq", 0, 0, tiled=True).reshape(
        seq_count, own_adapters, CAP, feat_width
    )
    key_rows = shape_query(key_lin.reshape(tok_count, kv_heads, HD), key_gain, positions).astype(
        jnp.bfloat16
    )
    values = value_lin.astype(jnp.bfloat16).reshape(tok_count, kv_heads, HD)
    rim_count = WINDOW // tok_count
    key_list = []
    value_list = []
    doc_list = []
    place_list = []
    kv_rows = jnp.stack([key_rows, values], axis=1)
    for distance in range(rim_count, 0, -1):
        far_kv, far_docs = passed_along((kv_rows, doc_ids), "seq", distance)
        key_list.append(far_kv[:, 0])
        value_list.append(far_kv[:, 1])
        doc_list.append(far_docs)
        place_list.append(positions - distance * tok_count)
    key_list.append(key_rows)
    value_list.append(values)
    doc_list.append(doc_ids)
    place_list.append(positions)
    window_keys = jnp.concatenate(key_list, axis=0)
    window_values = jnp.concatenate(value_list, axis=0)
    key_docs = jnp.concatenate(doc_list, axis=0)
    key_pos = jnp.concatenate(place_list, axis=0)
    key_gap = positions[:, None] - key_pos[None, :]
    allowed = (
        (doc_ids[:, None] == key_docs[None, :])
        & (key_gap >= 0)
        & (key_gap < WINDOW)
        & (key_pos[None, :] >= 0)
    )
    arrived, query_lin, window_keys, window_values, allowed = lax.optimization_barrier(
        (arrived, query_lin, window_keys, window_values, allowed)
    )
    partial_low = jnp.einsum(
        "sacd,ard->sacr", arrived, adapter_down, preferred_element_type=jnp.float32
    )
    slot_low = lax.psum(partial_low, "tensor").astype(jnp.bfloat16)
    all_up = lax.all_gather(adapter_up, "seq", axis=0, tiled=True)
    back_low = lax.all_to_all(
        slot_low.reshape(seq_count * own_adapters * CAP, R), "seq", 0, 0, tiled=True
    ).reshape(ADAPTERS, CAP, R)
    slot_lift = jnp.einsum(
        "acr,are->ace", back_low, all_up, preferred_element_type=jnp.float32
    ).astype(jnp.bfloat16)
    lifted = jnp.einsum(
        "st,se->te",
        dispatch,
        slot_lift.reshape(ADAPTERS * CAP, q_width),
        preferred_element_type=jnp.float32,
    ).astype(jnp.bfloat16)
    query_pre = (query_lin + lifted.astype(jnp.float32)).reshape(tok_count, local_heads, HD)
    queries, query_back = jax.vjp(
        lambda pre_query: shape_query(pre_query, query_gain, positions), query_pre
    )
    queries = queries.astype(jnp.bfloat16).reshape(tok_count, kv_heads, head_group, HD)
    upstream = cotangent.reshape(tok_count, kv_heads, head_group, HD)
    block_out, dqueries = attend(queries, window_keys, window_values, upstream, allowed)
    attended = block_out.reshape(tok_count, q_width)
    (dquery_pre,) = query_back(dqueries.reshape(tok_count, local_heads, HD))
    dquery_pre = dquery_pre.reshape(tok_count, q_width).astype(jnp.bfloat16)
    out_grad = jnp.dot(dispatch, dquery_pre, preferred_element_type=jnp.float32).astype(
        jnp.bfloat16
    )
    grad_rows = lax.all_to_all(out_grad, "seq", 0, 0, tiled=True).reshape(
        seq_count, own_adapters, CAP, q_width
    )
    grad_up = jnp.einsum(
        "sacr,sace->are", slot_low, grad_rows, preferred_element_type=jnp.float32
    )
    return (attended, grad_up)


def solution(mesh):
    in_specs = (
        P("seq", "tensor"),
        P(None, "tensor"),
        P(None, "tensor"),
        P(None, "tensor"),
        P(),
        P(),
        P("seq", None, "tensor"),
        P("seq", None, "tensor"),
        P("seq", None),
        P("seq"),
        P("seq", "tensor"),
    )
    out_specs = (P("seq", "tensor"), P("seq", None, "tensor"))
    return jax.shard_map(local, mesh=mesh, in_specs=in_specs, out_specs=out_specs, check_vma=False)
```

```python
import math

import jax
import jax.numpy as jnp
from jax import lax
from jax.sharding import PartitionSpec as P

HD = 256
R = 64
WINDOW = 1024
ADAPTERS = 64
CAP = 16


def passed_along(value, axis, steps):
    count = lax.axis_size(axis)
    first, last = (max(0, -steps), min(count, count - steps))
    return lax.ppermute(value, axis, [(source, source + steps) for source in range(first, last)])


def normalize(pre_field, gain_vec):
    mean_sq = jnp.mean(pre_field * pre_field, axis=-1, keepdims=True)
    return pre_field * lax.rsqrt(mean_sq + 1e-06) * gain_vec


def rotate(pre_field, positions):
    half_dim = pre_field.shape[-1] // 2
    frequency = jnp.exp(
        jnp.arange(half_dim, dtype=jnp.float32) * (-2.0 * math.log(10000.0) / pre_field.shape[-1])
    )
    angles = positions.astype(jnp.float32)[:, None] * frequency[None, :]
    cosine = jnp.cos(angles)[:, None, :]
    sine_part = jnp.sin(angles)[:, None, :]
    lower_half = pre_field[..., :half_dim]
    second = pre_field[..., half_dim:]
    return jnp.concatenate(
        [lower_half * cosine - second * sine_part, second * cosine + lower_half * sine_part],
        axis=-1,
    )


def shape_query(pre_field, gain_vec, positions):
    return rotate(normalize(pre_field, gain_vec), positions)


def attend(queries, key_rows, values, upstream, allowed):
    score_scale = 1.0 / math.sqrt(queries.shape[-1])
    scores = (
        jnp.einsum("tngd,knd->ngtk", queries, key_rows, preferred_element_type=jnp.float32)
        * score_scale
    )
    weights = jnp.where(allowed[None, None], jnp.exp(scores), 0.0)
    probs = weights / jnp.sum(weights, axis=-1, keepdims=True)
    probs_low = probs.astype(jnp.bfloat16)
    attended = jnp.einsum("ngtk,knd->tngd", probs_low, values, preferred_element_type=jnp.float32)
    dprobs = jnp.einsum("tngd,knd->ngtk", upstream, values, preferred_element_type=jnp.float32)
    delta = jnp.sum(probs * dprobs, axis=-1, keepdims=True)
    dscores = (probs * (dprobs - delta) * score_scale).astype(jnp.bfloat16)
    dqueries = jnp.einsum("ngtk,knd->tngd", dscores, key_rows, preferred_element_type=jnp.float32)
    return (attended.astype(jnp.bfloat16), dqueries)


def local(
    tokens,
    w_query,
    w_key,
    w_value,
    query_gain,
    key_gain,
    adapter_down,
    adapter_up,
    adapter_ids,
    doc_ids,
    cotangent,
):
    tok_count = tokens.shape[0]
    feat_width = tokens.shape[1]
    q_width = w_query.shape[1]
    kv_width = w_key.shape[1]
    local_heads = q_width // HD
    kv_heads = kv_width // HD
    head_group = local_heads // kv_heads
    positions = lax.axis_index("seq") * tok_count + jnp.arange(tok_count, dtype=jnp.int32)
    shard_cols = lax.all_gather(tokens, "tensor", axis=1, tiled=True)
    query_lin = jnp.dot(shard_cols, w_query, preferred_element_type=jnp.float32)
    key_lin = jnp.dot(shard_cols, w_key, preferred_element_type=jnp.float32)
    value_lin = jnp.dot(shard_cols, w_value, preferred_element_type=jnp.float32)
    token_adapter = adapter_ids[:, 0]
    chosen = token_adapter[:, None] == jnp.arange(ADAPTERS, dtype=jnp.int32)[None, :]
    before = jnp.cumsum(chosen.astype(jnp.int32), axis=0) - 1
    slot_rank = jnp.sum(jnp.where(chosen, before, 0), axis=1)
    slot_index = token_adapter * CAP + slot_rank
    dispatch = (slot_index[None, :] == jnp.arange(ADAPTERS * CAP, dtype=jnp.int32)[:, None]).astype(
        jnp.bfloat16
    )
    dispatch_t = (slot_index[:, None] == jnp.arange(ADAPTERS * CAP, dtype=jnp.int32)[None, :]).astype(
        jnp.bfloat16
    )
    outgoing = jnp.einsum(
        "ts,td->sd", dispatch_t, tokens, preferred_element_type=jnp.bfloat16
    )
    seq_count = lax.axis_size("seq")
    own_adapters = adapter_down.shape[0]
    arrived = lax.all_to_all(outgoing, "seq", 0, 0, tiled=True).reshape(
        seq_count, own_adapters, CAP, feat_width
    )
    key_rows = shape_query(key_lin.reshape(tok_count, kv_heads, HD), key_gain, positions).astype(
        jnp.bfloat16
    )
    values = value_lin.astype(jnp.bfloat16).reshape(tok_count, kv_heads, HD)
    rim_count = WINDOW // tok_count
    key_list = []
    value_list = []
    doc_list = []
    place_list = []
    kv_rows = jnp.stack([key_rows, values], axis=1)
    for distance in range(rim_count, 0, -1):
        far_kv, far_docs = passed_along((kv_rows, doc_ids), "seq", distance)
        key_list.append(far_kv[:, 0])
        value_list.append(far_kv[:, 1])
        doc_list.append(far_docs)
        place_list.append(positions - distance * tok_count)
    key_list.append(key_rows)
    value_list.append(values)
    doc_list.append(doc_ids)
    place_list.append(positions)
    window_keys = jnp.concatenate(key_list, axis=0)
    window_values = jnp.concatenate(value_list, axis=0)
    key_docs = jnp.concatenate(doc_list, axis=0)
    key_pos = jnp.concatenate(place_list, axis=0)
    key_gap = positions[:, None] - key_pos[None, :]
    allowed = (
        (doc_ids[:, None] == key_docs[None, :])
        & (key_gap >= 0)
        & (key_gap < WINDOW)
        & (key_pos[None, :] >= 0)
    )
    arrived, query_lin, window_keys, window_values, allowed = lax.optimization_barrier(
        (arrived, query_lin, window_keys, window_values, allowed)
    )
    partial_low = jnp.einsum(
        "sacd,ard->sacr", arrived, adapter_down, preferred_element_type=jnp.float32
    )
    slot_low = jnp.sum(lax.all_gather(partial_low, "tensor"), axis=0).astype(jnp.bfloat16)
    slot_lift = jnp.einsum(
        "sacr,are->sace", slot_low, adapter_up, preferred_element_type=jnp.float32
    ).astype(jnp.bfloat16)
    back_lift = lax.all_to_all(
        slot_lift.reshape(seq_count * own_adapters * CAP, q_width), "seq", 0, 0, tiled=True
    )
    lifted = jnp.einsum(
        "st,se->te",
        dispatch,
        back_lift,
        preferred_element_type=jnp.float32,
    ).astype(jnp.bfloat16)
    query_pre = (query_lin + lifted.astype(jnp.float32)).reshape(tok_count, local_heads, HD)
    queries, query_back = jax.vjp(
        lambda pre_query: shape_query(pre_query, query_gain, positions), query_pre
    )
    queries = queries.astype(jnp.bfloat16).reshape(tok_count, kv_heads, head_group, HD)
    upstream = cotangent.reshape(tok_count, kv_heads, head_group, HD)
    block_out, dqueries = attend(queries, window_keys, window_values, upstream, allowed)
    attended = block_out.reshape(tok_count, q_width)
    (dquery_pre,) = query_back(dqueries.reshape(tok_count, local_heads, HD))
    dquery_pre = dquery_pre.reshape(tok_count, q_width).astype(jnp.bfloat16)
    out_grad = jnp.dot(dispatch, dquery_pre, preferred_element_type=jnp.float32).astype(
        jnp.bfloat16
    )
    grad_rows = lax.all_to_all(out_grad, "seq", 0, 0, tiled=True).reshape(
        seq_count, own_adapters, CAP, q_width
    )
    grad_up = jnp.einsum(
        "sacr,sace->are", slot_low, grad_rows, preferred_element_type=jnp.float32
    )
    return (attended, grad_up)


def solution(mesh):
    in_specs = (
        P("seq", "tensor"),
        P(None, "tensor"),
        P(None, "tensor"),
        P(None, "tensor"),
        P(),
        P(),
        P("seq", None, "tensor"),
        P("seq", None, "tensor"),
        P("seq", None),
        P("seq"),
        P("seq", "tensor"),
    )
    out_specs = (P("seq", "tensor"), P("seq", None, "tensor"))
    return jax.shard_map(local, mesh=mesh, in_specs=in_specs, out_specs=out_specs, check_vma=False)
```

```python
import math

import jax
import jax.numpy as jnp
from jax import lax
from jax.sharding import PartitionSpec as P

HD = 256
R = 64
WINDOW = 1024
ADAPTERS = 64
CAP = 16


def passed_along(value, axis, steps):
    count = lax.axis_size(axis)
    first, last = (max(0, -steps), min(count, count - steps))
    return lax.ppermute(value, axis, [(source, source + steps) for source in range(first, last)])


def normalize(pre_field, gain_vec):
    mean_sq = jnp.mean(pre_field * pre_field, axis=-1, keepdims=True)
    return pre_field * lax.rsqrt(mean_sq + 1e-06) * gain_vec


def rotate(pre_field, positions):
    half_dim = pre_field.shape[-1] // 2
    frequency = jnp.exp(
        jnp.arange(half_dim, dtype=jnp.float32) * (-2.0 * math.log(10000.0) / pre_field.shape[-1])
    )
    angles = positions.astype(jnp.float32)[:, None] * frequency[None, :]
    cosine = jnp.cos(angles)[:, None, :]
    sine_part = jnp.sin(angles)[:, None, :]
    lower_half = pre_field[..., :half_dim]
    second = pre_field[..., half_dim:]
    return jnp.concatenate(
        [lower_half * cosine - second * sine_part, second * cosine + lower_half * sine_part],
        axis=-1,
    )


def shape_query(pre_field, gain_vec, positions):
    return rotate(normalize(pre_field, gain_vec), positions)


def attend(queries, key_rows, values, upstream, allowed):
    score_scale = 1.0 / math.sqrt(queries.shape[-1])
    scores = (
        jnp.einsum("tngd,knd->ngtk", queries, key_rows, preferred_element_type=jnp.float32)
        * score_scale
    )
    weights = jnp.where(allowed[None, None], jnp.exp(scores), 0.0)
    probs = weights / jnp.sum(weights, axis=-1, keepdims=True)
    probs_low = probs.astype(jnp.bfloat16)
    attended = jnp.einsum("ngtk,knd->tngd", probs_low, values, preferred_element_type=jnp.float32)
    dprobs = jnp.einsum("tngd,knd->ngtk", upstream, values, preferred_element_type=jnp.float32)
    delta = jnp.sum(probs * dprobs, axis=-1, keepdims=True)
    dscores = (probs * (dprobs - delta) * score_scale).astype(jnp.bfloat16)
    dqueries = jnp.einsum("ngtk,knd->tngd", dscores, key_rows, preferred_element_type=jnp.float32)
    return (attended.astype(jnp.bfloat16), dqueries)


def local(
    tokens,
    w_query,
    w_key,
    w_value,
    query_gain,
    key_gain,
    adapter_down,
    adapter_up,
    adapter_ids,
    doc_ids,
    cotangent,
):
    tok_count = tokens.shape[0]
    feat_width = tokens.shape[1]
    q_width = w_query.shape[1]
    kv_width = w_key.shape[1]
    local_heads = q_width // HD
    kv_heads = kv_width // HD
    head_group = local_heads // kv_heads
    positions = lax.axis_index("seq") * tok_count + jnp.arange(tok_count, dtype=jnp.int32)
    shard_cols = lax.all_gather(tokens, "tensor", axis=1, tiled=True)
    query_lin = jnp.dot(shard_cols, w_query, preferred_element_type=jnp.float32)
    key_lin = jnp.dot(shard_cols, w_key, preferred_element_type=jnp.float32)
    value_lin = jnp.dot(shard_cols, w_value, preferred_element_type=jnp.float32)
    token_adapter = adapter_ids[:, 0]
    chosen = token_adapter[:, None] == jnp.arange(ADAPTERS, dtype=jnp.int32)[None, :]
    before = jnp.cumsum(chosen.astype(jnp.int32), axis=0) - 1
    slot_rank = jnp.sum(jnp.where(chosen, before, 0), axis=1)
    slot_index = token_adapter * CAP + slot_rank
    dispatch = (slot_index[None, :] == jnp.arange(ADAPTERS * CAP, dtype=jnp.int32)[:, None]).astype(
        jnp.bfloat16
    )
    dispatch_t = (slot_index[:, None] == jnp.arange(ADAPTERS * CAP, dtype=jnp.int32)[None, :]).astype(
        jnp.bfloat16
    )
    outgoing = jnp.einsum(
        "ts,td->sd", dispatch_t, tokens, preferred_element_type=jnp.bfloat16
    )
    seq_count = lax.axis_size("seq")
    own_adapters = adapter_down.shape[0]
    arrived = lax.all_to_all(outgoing, "seq", 0, 0, tiled=True).reshape(
        seq_count, own_adapters, CAP, feat_width
    )
    key_rows = shape_query(key_lin.reshape(tok_count, kv_heads, HD), key_gain, positions).astype(
        jnp.bfloat16
    )
    values = value_lin.astype(jnp.bfloat16).reshape(tok_count, kv_heads, HD)
    rim_count = WINDOW // tok_count
    key_list = []
    value_list = []
    doc_list = []
    place_list = []
    kv_rows = jnp.concatenate(
        [
            jnp.stack([key_rows, values], axis=0).reshape(2 * tok_count, HD),
            doc_ids.astype(jnp.bfloat16).reshape(-1, HD),
        ],
        axis=0,
    )
    for distance in range(rim_count, 0, -1):
        far_kv = passed_along(kv_rows, "seq", distance)
        key_list.append(far_kv[:tok_count].reshape(tok_count, kv_heads, HD))
        value_list.append(far_kv[tok_count : 2 * tok_count].reshape(tok_count, kv_heads, HD))
        doc_list.append(far_kv[2 * tok_count :].reshape(tok_count).astype(jnp.int32))
        place_list.append(positions - distance * tok_count)
    key_list.append(key_rows)
    value_list.append(values)
    doc_list.append(doc_ids)
    place_list.append(positions)
    window_keys = jnp.concatenate(key_list, axis=0)
    window_values = jnp.concatenate(value_list, axis=0)
    key_docs = jnp.concatenate(doc_list, axis=0)
    key_pos = jnp.concatenate(place_list, axis=0)
    key_gap = positions[:, None] - key_pos[None, :]
    allowed = (
        (doc_ids[:, None] == key_docs[None, :])
        & (key_gap >= 0)
        & (key_gap < WINDOW)
        & (key_pos[None, :] >= 0)
    )
    arrived, query_lin, window_keys, window_values, allowed = lax.optimization_barrier(
        (arrived, query_lin, window_keys, window_values, allowed)
    )
    partial_low = jnp.einsum(
        "sacd,ard->sacr", arrived, adapter_down, preferred_element_type=jnp.float32
    )
    slot_low = lax.psum(partial_low, "tensor").astype(jnp.bfloat16)
    all_up = lax.all_gather(adapter_up, "seq", axis=0, tiled=True)
    back_low = lax.all_to_all(
        slot_low.reshape(seq_count * own_adapters * CAP, R), "seq", 0, 0, tiled=True
    ).reshape(ADAPTERS, CAP, R)
    slot_lift = jnp.einsum(
        "acr,are->ace", back_low, all_up, preferred_element_type=jnp.float32
    ).astype(jnp.bfloat16)
    lifted = jnp.einsum(
        "st,se->te",
        dispatch,
        slot_lift.reshape(ADAPTERS * CAP, q_width),
        preferred_element_type=jnp.float32,
    ).astype(jnp.bfloat16)
    query_pre = (query_lin + lifted.astype(jnp.float32)).reshape(tok_count, local_heads, HD)
    queries, query_back = jax.vjp(
        lambda pre_query: shape_query(pre_query, query_gain, positions), query_pre
    )
    queries = queries.astype(jnp.bfloat16).reshape(tok_count, kv_heads, head_group, HD)
    upstream = cotangent.reshape(tok_count, kv_heads, head_group, HD)
    block_out, dqueries = attend(queries, window_keys, window_values, upstream, allowed)
    attended = block_out.reshape(tok_count, q_width)
    (dquery_pre,) = query_back(dqueries.reshape(tok_count, local_heads, HD))
    dquery_pre = dquery_pre.reshape(tok_count, q_width).astype(jnp.bfloat16)
    out_grad = jnp.dot(dispatch, dquery_pre, preferred_element_type=jnp.float32).astype(
        jnp.bfloat16
    )
    grad_rows = lax.all_to_all(out_grad, "seq", 0, 0, tiled=True).reshape(
        seq_count, own_adapters, CAP, q_width
    )
    grad_up = jnp.einsum(
        "sacr,sace->are", slot_low, grad_rows, preferred_element_type=jnp.float32
    )
    return (attended, grad_up)


def solution(mesh):
    in_specs = (
        P("seq", "tensor"),
        P(None, "tensor"),
        P(None, "tensor"),
        P(None, "tensor"),
        P(),
        P(),
        P("seq", None, "tensor"),
        P("seq", None, "tensor"),
        P("seq", None),
        P("seq"),
        P("seq", "tensor"),
    )
    out_specs = (P("seq", "tensor"), P("seq", None, "tensor"))
    return jax.shard_map(local, mesh=mesh, in_specs=in_specs, out_specs=out_specs, check_vma=False)
```

```python
import math

import jax
import jax.numpy as jnp
from jax import lax
from jax.sharding import PartitionSpec as P

HD = 256
R = 64
WINDOW = 1024
ADAPTERS = 64
CAP = 16


def passed_along(value, axis, steps):
    count = lax.axis_size(axis)
    first, last = (max(0, -steps), min(count, count - steps))
    return lax.ppermute(value, axis, [(source, source + steps) for source in range(first, last)])


def normalize(pre_field, gain_vec):
    mean_sq = jnp.mean(pre_field * pre_field, axis=-1, keepdims=True)
    return pre_field * lax.rsqrt(mean_sq + 1e-06) * gain_vec


def rotate(pre_field, positions):
    half_dim = pre_field.shape[-1] // 2
    frequency = jnp.exp(
        jnp.arange(half_dim, dtype=jnp.float32) * (-2.0 * math.log(10000.0) / pre_field.shape[-1])
    )
    angles = positions.astype(jnp.float32)[:, None] * frequency[None, :]
    cosine = jnp.cos(angles)[:, None, :]
    sine_part = jnp.sin(angles)[:, None, :]
    lower_half = pre_field[..., :half_dim]
    second = pre_field[..., half_dim:]
    return jnp.concatenate(
        [lower_half * cosine - second * sine_part, second * cosine + lower_half * sine_part],
        axis=-1,
    )


def shape_query(pre_field, gain_vec, positions):
    return rotate(normalize(pre_field, gain_vec), positions)


def attend(queries, key_rows, values, upstream, allowed):
    score_scale = 1.0 / math.sqrt(queries.shape[-1])
    scores = (
        jnp.einsum("tngd,knd->ngtk", queries, key_rows, preferred_element_type=jnp.float32)
        * score_scale
    )
    weights = jnp.where(allowed[None, None], jnp.exp(scores), 0.0)
    probs = weights / jnp.sum(weights, axis=-1, keepdims=True)
    probs_low = probs.astype(jnp.bfloat16)
    attended = jnp.einsum("ngtk,knd->tngd", probs_low, values, preferred_element_type=jnp.float32)
    dprobs = jnp.einsum("tngd,knd->ngtk", upstream, values, preferred_element_type=jnp.float32)
    delta = jnp.sum(probs * dprobs, axis=-1, keepdims=True)
    dscores = (probs * (dprobs - delta) * score_scale).astype(jnp.bfloat16)
    dqueries = jnp.einsum("ngtk,knd->tngd", dscores, key_rows, preferred_element_type=jnp.float32)
    return (attended.astype(jnp.bfloat16), dqueries)


def local(
    tokens,
    w_query,
    w_key,
    w_value,
    query_gain,
    key_gain,
    adapter_down,
    adapter_up,
    adapter_ids,
    doc_ids,
    cotangent,
):
    tok_count = tokens.shape[0]
    feat_width = tokens.shape[1]
    q_width = w_query.shape[1]
    kv_width = w_key.shape[1]
    local_heads = q_width // HD
    kv_heads = kv_width // HD
    head_group = local_heads // kv_heads
    positions = lax.axis_index("seq") * tok_count + jnp.arange(tok_count, dtype=jnp.int32)
    shard_cols = lax.all_gather(tokens, "tensor", axis=1, tiled=True)
    query_lin = jnp.dot(shard_cols, w_query, preferred_element_type=jnp.float32)
    key_lin = jnp.dot(shard_cols, w_key, preferred_element_type=jnp.float32)
    value_lin = jnp.dot(shard_cols, w_value, preferred_element_type=jnp.float32)
    token_adapter = adapter_ids[:, 0]
    chosen = token_adapter[:, None] == jnp.arange(ADAPTERS, dtype=jnp.int32)[None, :]
    earlier = (
        jnp.arange(tok_count, dtype=jnp.int32)[:, None] > jnp.arange(tok_count, dtype=jnp.int32)[None, :]
    ).astype(jnp.bfloat16)
    before = jnp.dot(
        earlier, chosen.astype(jnp.bfloat16), preferred_element_type=jnp.float32
    ).astype(jnp.int32)
    slot_rank = jnp.sum(jnp.where(chosen, before, 0), axis=1)
    slot_index = token_adapter * CAP + slot_rank
    dispatch = (slot_index[None, :] == jnp.arange(ADAPTERS * CAP, dtype=jnp.int32)[:, None]).astype(
        jnp.bfloat16
    )
    dispatch_t = (slot_index[:, None] == jnp.arange(ADAPTERS * CAP, dtype=jnp.int32)[None, :]).astype(
        jnp.bfloat16
    )
    outgoing = jnp.einsum(
        "ts,td->sd", dispatch_t, tokens, preferred_element_type=jnp.bfloat16
    )
    seq_count = lax.axis_size("seq")
    own_adapters = adapter_down.shape[0]
    arrived = lax.all_to_all(outgoing, "seq", 0, 0, tiled=True).reshape(
        seq_count, own_adapters, CAP, feat_width
    )
    key_rows = shape_query(key_lin.reshape(tok_count, kv_heads, HD), key_gain, positions).astype(
        jnp.bfloat16
    )
    values = value_lin.astype(jnp.bfloat16).reshape(tok_count, kv_heads, HD)
    rim_count = WINDOW // tok_count
    key_list = []
    value_list = []
    doc_list = []
    place_list = []
    kv_rows = jnp.stack([key_rows, values], axis=1)
    for distance in range(rim_count, 0, -1):
        far_kv, far_docs = passed_along((kv_rows, doc_ids), "seq", distance)
        key_list.append(far_kv[:, 0])
        value_list.append(far_kv[:, 1])
        doc_list.append(far_docs)
        place_list.append(positions - distance * tok_count)
    key_list.append(key_rows)
    value_list.append(values)
    doc_list.append(doc_ids)
    place_list.append(positions)
    window_keys = jnp.concatenate(key_list, axis=0)
    window_values = jnp.concatenate(value_list, axis=0)
    key_docs = jnp.concatenate(doc_list, axis=0)
    key_pos = jnp.concatenate(place_list, axis=0)
    key_gap = positions[:, None] - key_pos[None, :]
    allowed = (
        (doc_ids[:, None] == key_docs[None, :])
        & (key_gap >= 0)
        & (key_gap < WINDOW)
        & (key_pos[None, :] >= 0)
    )
    arrived, query_lin, window_keys, window_values, allowed = lax.optimization_barrier(
        (arrived, query_lin, window_keys, window_values, allowed)
    )
    partial_low = jnp.einsum(
        "sacd,ard->sacr", arrived, adapter_down, preferred_element_type=jnp.float32
    )
    slot_low = lax.psum(partial_low, "tensor").astype(jnp.bfloat16)
    all_up = lax.all_gather(adapter_up, "seq", axis=0, tiled=True)
    back_low = lax.all_to_all(
        slot_low.reshape(seq_count * own_adapters * CAP, R), "seq", 0, 0, tiled=True
    ).reshape(ADAPTERS, CAP, R)
    slot_lift = jnp.einsum(
        "acr,are->ace", back_low, all_up, preferred_element_type=jnp.float32
    ).astype(jnp.bfloat16)
    lifted = jnp.einsum(
        "st,se->te",
        dispatch,
        slot_lift.reshape(ADAPTERS * CAP, q_width),
        preferred_element_type=jnp.float32,
    ).astype(jnp.bfloat16)
    query_pre = (query_lin + lifted.astype(jnp.float32)).reshape(tok_count, local_heads, HD)
    queries, query_back = jax.vjp(
        lambda pre_query: shape_query(pre_query, query_gain, positions), query_pre
    )
    queries = queries.astype(jnp.bfloat16).reshape(tok_count, kv_heads, head_group, HD)
    upstream = cotangent.reshape(tok_count, kv_heads, head_group, HD)
    block_out, dqueries = attend(queries, window_keys, window_values, upstream, allowed)
    attended = block_out.reshape(tok_count, q_width)
    (dquery_pre,) = query_back(dqueries.reshape(tok_count, local_heads, HD))
    dquery_pre = dquery_pre.reshape(tok_count, q_width).astype(jnp.bfloat16)
    out_grad = jnp.dot(dispatch, dquery_pre, preferred_element_type=jnp.float32).astype(
        jnp.bfloat16
    )
    grad_rows = lax.all_to_all(out_grad, "seq", 0, 0, tiled=True).reshape(
        seq_count, own_adapters, CAP, q_width
    )
    grad_up = jnp.einsum(
        "sacr,sace->are", slot_low, grad_rows, preferred_element_type=jnp.float32
    )
    return (attended, grad_up)


def solution(mesh):
    in_specs = (
        P("seq", "tensor"),
        P(None, "tensor"),
        P(None, "tensor"),
        P(None, "tensor"),
        P(),
        P(),
        P("seq", None, "tensor"),
        P("seq", None, "tensor"),
        P("seq", None),
        P("seq"),
        P("seq", "tensor"),
    )
    out_specs = (P("seq", "tensor"), P("seq", None, "tensor"))
    return jax.shard_map(local, mesh=mesh, in_specs=in_specs, out_specs=out_specs, check_vma=False)
```
